512 devices in a mesh: chain: 64 (over x, y, z_hi, core), block: 8 (over z_lo).
Axes of the slice: x: 4, y: 4, z: 16 (z_hi: 2, z_lo: 8; z = z_hi * 8 + z_lo), core: 2. Of those that a mesh axis runs over, the one named last changes fastest.
Arguments:
- site_tensors: bfloat16 [64, 32, 2, 256, 256], P('chain', 'block'), may hold values from -4.5 to 7.5
- sketch: bfloat16 [512, 256], replicated, may hold values from -6 to 6
- bond_sizes: int32 [64, 2, 32], P('chain'), may hold values from 32 to 256, as said below
- kept_ranks: int32 [64, 2, 32], P('chain'), may hold values from 0 to 256, as said below
- couplings: float32 [64, 2, 3], P('chain'), may hold values from -1 to 2.5, as said below
Outputs:
- updated_sites: bfloat16 [64, 32, 2, 256, 256], P('chain', 'block')
The draws below stay inside these ranges and needn't reach their ends.
Inputs may be any that keep to these rules, and one draw needn't show every extreme that they name: bond_sizes[i, 1] are the block sizes of the bond right of site i and bond_sizes[i, 0] equals bond_sizes[i - 1 mod 64, 1]; every bond has a block of exactly 256. kept_ranks[i, 1] belongs to the bond right of site i and kept_ranks[i, 0] equals kept_ranks[i - 1 mod 64, 1]; a count never exceeds that block's size; some block keeps exactly 256. couplings[i, 0] equals couplings[i - 1 mod 64, 1]; hopping lies in 0.5 to 2.5, the other two in -1 to 1.
All inputs are finite; a program needn't handle non-finite values.
Results may differ from the reference program's by a relative error of at most 0.035.
Values may be sent and summed in bfloat16 or wider, within the bound.
A program may use at most 64 MiB of HBM per device.

```python
import jax
import jax.numpy as jnp
from jax import lax

P_SIZE = 256
SECTORS = 32
RMAX = 256
SITES = 64


def pair_sum_down(values):
    return values + jnp.concatenate([jnp.zeros((values.shape[0], 1), jnp.int32), values[:, :-1]], axis=1)


def pair_sum_up(values):
    return values + jnp.concatenate([values[:, 1:], jnp.zeros((values.shape[0], 1), jnp.int32)], axis=1)


def bond_layout(key):
    base_key = jax.random.fold_in(key, 7)
    key_center, key_slope, key_cap = jax.random.split(base_key, 3)
    center = jax.random.randint(key_center, (), 1, SECTORS - 1)
    slope_step = jax.random.randint(key_slope, (SITES, 1), 1 + P_SIZE // 64, 2 + P_SIZE // 10)
    sector = jnp.arange(SECTORS, dtype=jnp.int32)[None, :]
    distance = jnp.maximum(jnp.abs(sector - center) - 1, 0)
    block_sizes = jnp.maximum(max(1, P_SIZE // 8), P_SIZE - slope_step * distance).astype(jnp.int32)
    rank_cap = jax.random.randint(key_cap, (SITES, SECTORS), RMAX // 2, RMAX + 1)
    rank_cap = jnp.where(sector == center, RMAX, rank_cap).astype(jnp.int32)
    previous = jnp.roll(block_sizes, 1, axis=0)
    following = jnp.roll(block_sizes, -1, axis=0)
    rank_bound = jnp.minimum(block_sizes, jnp.minimum(pair_sum_down(previous), pair_sum_up(following)) // 2)
    even_rank = jnp.minimum(rank_cap, rank_bound)
    rank_prev = jnp.roll(even_rank, 1, axis=0)
    rank_next = jnp.roll(even_rank, -1, axis=0)
    odd_bound = jnp.minimum(block_sizes, jnp.minimum(pair_sum_down(rank_prev), pair_sum_up(rank_next)) // 2)
    odd_rank = jnp.minimum(rank_cap, odd_bound)
    is_even = jnp.arange(SITES, dtype=jnp.int32)[:, None] % 2 == 0
    bond_rank = jnp.where(is_even, even_rank, odd_rank).astype(jnp.int32)
    return (block_sizes, bond_rank)


def draw_bond_sizes(key, part):
    block_sizes, bond_rank = bond_layout(key)
    return jnp.stack([jnp.roll(block_sizes, 1, axis=0), block_sizes], axis=1)


def draw_kept_ranks(key, part):
    block_sizes, bond_rank = bond_layout(key)
    return jnp.stack([jnp.roll(bond_rank, 1, axis=0), bond_rank], axis=1)


def draw_couplings(key, part):
    uniform_draw = jax.random.uniform(jax.random.fold_in(key, 11), (SITES, 3), jnp.float32)
    lower_end = jnp.array([0.5, -1.0, -1.0], jnp.float32)
    upper_end = jnp.array([2.5, 1.0, 1.0], jnp.float32)
    bond_terms = lower_end + (upper_end - lower_end) * uniform_draw
    return jnp.stack([jnp.roll(bond_terms, 1, axis=0), bond_terms], axis=1)


def draw_site_tensors(key, part):
    block_sizes, bond_rank = bond_layout(key)
    left_sizes = jnp.roll(block_sizes, 1, axis=0)
    right_next = jnp.concatenate([block_sizes[:, 1:], jnp.zeros((SITES, 1), jnp.int32)], axis=1)
    noise_draw = jax.random.normal(jax.random.fold_in(key, 13), (SITES, SECTORS, 2, P_SIZE, P_SIZE), jnp.float32)
    noise_draw = jnp.clip(noise_draw, -5.0, 5.0)
    extent_zero = jnp.maximum(jnp.maximum(left_sizes, block_sizes), 1).astype(jnp.float32)
    extent_one = jnp.maximum(jnp.maximum(left_sizes, right_next), 1).astype(jnp.float32)
    extent = jnp.stack([extent_zero, extent_one], axis=2)
    spread = 0.9 / jnp.sqrt(extent)
    diagonal = 3.0 * jnp.eye(P_SIZE, dtype=jnp.float32)
    return (diagonal + spread[..., None, None] * noise_draw).astype(jnp.bfloat16)


def scatter_about(key, shape, scale, bound, held_as=jnp.bfloat16):
    drawn = scale * jax.random.normal(key, shape, jnp.float32)
    return jnp.clip(drawn, min=-bound, max=bound).astype(held_as)


def setup_inputs(seed: int = 0) -> dict:
    key_of = jax.random.split(jax.random.key(seed), 6)
    return {
        "site_tensors": draw_site_tensors(jax.random.fold_in(key_of[5], 71), 0),
        "sketch": scatter_about(key_of[1], (2 * P_SIZE, RMAX), 1.0, 6.0),
        "bond_sizes": draw_bond_sizes(jax.random.fold_in(key_of[5], 71), 0),
        "kept_ranks": draw_kept_ranks(jax.random.fold_in(key_of[5], 71), 0),
        "couplings": draw_couplings(jax.random.fold_in(key_of[5], 71), 0),
    }


tau_step = 0.5

def gate_terms(coupling):
    hopping = coupling[0]
    ising_term = coupling[1]
    field_term = coupling[2]
    rotation = 0.5 * tau_step * hopping
    middle_scale = jnp.exp(0.25 * tau_step * ising_term)
    weight_empty = jnp.exp(-tau_step * (0.25 * ising_term - 0.5 * field_term))
    weight_full = jnp.exp(-tau_step * (0.25 * ising_term + 0.5 * field_term))
    weight_stay = middle_scale * jnp.cosh(rotation)
    weight_swap = -middle_scale * jnp.sinh(rotation)
    return (weight_empty, weight_stay, weight_swap, weight_full)

def mask_site(site_block, left_sizes, right_sizes):
    row_index = jnp.arange(P_SIZE, dtype=jnp.int32)
    right_next = jnp.concatenate([right_sizes[1:], jnp.zeros((1,), jnp.int32)])
    row_keep = row_index[None, :] < left_sizes[:, None]
    col_stay = row_index[None, :] < right_sizes[:, None]
    col_next = row_index[None, :] < right_next[:, None]
    keep_zero = row_keep[:, :, None] & col_stay[:, None, :]
    keep_one = row_keep[:, :, None] & col_next[:, None, :]
    keep_both = jnp.stack([keep_zero, keep_one], axis=1)
    return jnp.where(keep_both, site_block, jnp.zeros_like(site_block))

def widen(values):
    return values.astype(jnp.float32)

def round_product(left_part, right_part):
    return jnp.einsum('kij,kjl->kil', widen(left_part), widen(right_part)).astype(jnp.bfloat16)

def pair_update(left_site, right_site, mid_ranks, coupling, sketch):
    zero_block = jnp.zeros((1, P_SIZE, P_SIZE), jnp.bfloat16)
    left_zero = left_site[:, 0]
    left_one = left_site[:, 1]
    right_zero = right_site[:, 0]
    right_one = right_site[:, 1]
    left_below = jnp.concatenate([zero_block, left_one[:-1]], axis=0)
    stay_stay = round_product(left_zero, right_zero)
    stay_up = round_product(left_zero, right_one)
    up_stay = round_product(left_below, right_zero)
    up_up = round_product(left_below, right_one)
    up_stay_next = jnp.concatenate([up_stay[1:], zero_block], axis=0)
    stay_up_prev = jnp.concatenate([zero_block, stay_up[:-1]], axis=0)
    weight_empty, weight_stay, weight_swap, weight_full = gate_terms(coupling)
    top_left = weight_empty * widen(stay_stay)
    top_right = weight_stay * widen(stay_up) + weight_swap * widen(up_stay_next)
    bottom_left = weight_swap * widen(stay_up_prev) + weight_stay * widen(up_stay)
    bottom_right = weight_full * widen(up_up)
    two_site = jnp.concatenate([jnp.concatenate([top_left, top_right], axis=2), jnp.concatenate([bottom_left, bottom_right], axis=2)], axis=1).astype(jnp.bfloat16)
    sample = jnp.einsum('kab,bc->kac', widen(two_site), widen(sketch))
    keep_mask = (jnp.arange(RMAX, dtype=jnp.int32)[None, :] < mid_ranks[:, None]).astype(jnp.float32)
    sample = sample * keep_mask[:, None, :]
    gram_matrix = jnp.einsum('kai,kaj->kij', sample, sample, precision=lax.Precision.HIGHEST)
    gram_matrix = gram_matrix + (1.0 - keep_mask)[:, :, None] * jnp.eye(RMAX, dtype=jnp.float32)[None]
    factor = jnp.linalg.cholesky(gram_matrix)
    solved = lax.linalg.triangular_solve(factor, sample, left_side=False, lower=True, transpose_a=True)
    basis_rows = (solved * jnp.sqrt(jnp.float32(P_SIZE))).astype(jnp.bfloat16)
    coef = jnp.einsum('kar,kab->krb', widen(basis_rows), widen(two_site))
    norm_total = jnp.sum(coef * coef)
    scaled = (coef * jnp.sqrt(jnp.float32(SECTORS * RMAX * P_SIZE) / norm_total)).astype(jnp.bfloat16)
    pad_count = P_SIZE - RMAX
    new_zero = jnp.pad(basis_rows[:, :P_SIZE, :], ((0, 0), (0, 0), (0, pad_count)))
    lower_part = jnp.pad(basis_rows[:, P_SIZE:, :], ((0, 0), (0, 0), (0, pad_count)))
    new_one = jnp.concatenate([lower_part[1:], zero_block], axis=0)
    new_left = jnp.stack([new_zero, new_one], axis=1)
    right_zero_new = jnp.pad(scaled[:, :, :P_SIZE], ((0, 0), (0, pad_count), (0, 0)))
    right_one_new = jnp.pad(scaled[:, :, P_SIZE:], ((0, 0), (0, pad_count), (0, 0)))
    new_right = jnp.stack([right_zero_new, right_one_new], axis=1)
    return (new_left, new_right)

def run_layer(current, left_index, right_index, kept_ranks, couplings, sketch):

    def update_pair(packed):
        left_site, right_site, mid_ranks, coupling = packed
        return pair_update(left_site, right_site, mid_ranks, coupling, sketch)
    new_left, new_right = lax.map(update_pair, (current[left_index], current[right_index], kept_ranks[left_index, 1], couplings[left_index, 1]))
    current = current.at[left_index].set(new_left)
    return current.at[right_index].set(new_right)

def reference(site_tensors, sketch, bond_sizes, kept_ranks, couplings):
    current = jax.vmap(mask_site)(site_tensors, bond_sizes[:, 0], bond_sizes[:, 1])
    even_left = jnp.arange(0, SITES, 2, dtype=jnp.int32)
    current = run_layer(current, even_left, even_left + 1, kept_ranks, couplings, sketch)
    odd_left = jnp.arange(1, SITES, 2, dtype=jnp.int32)
    current = run_layer(current, odd_left, (odd_left + 1) % SITES, kept_ranks, couplings, sketch)
    return current
```

```python
import functools
import math

import jax
import jax.numpy as jnp
from jax import lax
from jax.experimental import pallas as pl
from jax.experimental.pallas import tpu as pltpu
from jax.sharding import PartitionSpec as P

tau_step = 0.5
NN = (((1,), (0,)), ((), ()))
NT = (((1,), (1,)), ((), ()))


def mm(x, y, dims=NN):
    return lax.dot_general(x, y, dims, preferred_element_type=jnp.float32)


def split(x):
    high = x.astype(jnp.bfloat16)
    low = (x - high.astype(jnp.float32)).astype(jnp.bfloat16)
    return high, low


def mm3(x, y, dims=NN):
    x_high, x_low = split(x)
    y_high, y_low = split(y)
    return mm(x_high, y_high, dims) + (mm(x_high, y_low, dims) + mm(x_low, y_high, dims))


def inv_factors(blocks):
    nb = blocks[0].shape[0]
    ngr = nb // 8
    eye = (lax.broadcasted_iota(jnp.int32, (nb, nb), 0) == lax.broadcasted_iota(jnp.int32, (nb, nb), 1)).astype(jnp.float32)
    work = []
    for g in blocks:
        full = jnp.concatenate([g, eye], axis=1)
        work.append([full[8 * i: 8 * i + 8, :] for i in range(ngr)])
    lane = lax.broadcasted_iota(jnp.int32, (8, 2 * nb), 1)
    sub = lax.broadcasted_iota(jnp.int32, (8, 2 * nb), 0)
    for j in range(nb):
        gj, sj = j // 8, j % 8
        for w in work:
            row = w[gj][sj: sj + 1, :]
            piv = row[:, j: j + 1]
            t = row * (1.0 / piv)
            tb = jnp.broadcast_to(t, (8, 2 * nb))
            for i in range(gj, ngr):
                if i == gj and sj == 7:
                    continue
                c = jnp.broadcast_to(w[i][:, j: j + 1], (8, 2 * nb))
                if i == gj:
                    c = jnp.where(sub > sj, c, 0.0)
                w[i] = w[i] - c * tb
    out = []
    for w in work:
        rows = []
        for i in range(ngr):
            d = jnp.sum(jnp.where(lane == sub + 8 * i, w[i], 0.0), axis=1, keepdims=True)
            rows.append(w[i] * lax.rsqrt(d))
        full = jnp.concatenate(rows, axis=0)
        out.append(full[:, nb:])
    return out

def inv_cholesky(w_refs, nb=64, mmf=mm3):
    n = w_refs[0].shape[-1]
    for k in range(n // nb):
        lo, hi = k * nb, (k + 1) * nb
        xs = inv_factors([w[lo:hi, lo:hi] for w in w_refs])
        for w, x in zip(w_refs, xs):
            if hi < n:
                panel = mmf(w[hi:, lo:hi], x, NT)
                right = mmf(x, w[lo:hi, hi:])
            if lo > 0:
                left = jnp.concatenate([mmf(x, w[lo:hi, :lo]), x], axis=1)
            else:
                left = x
            w[lo:hi, :hi] = left
            if hi < n:
                w[lo:hi, hi:] = jnp.zeros((nb, n - hi), jnp.float32)
                w[hi:, hi:] = w[hi:, hi:] - mmf(panel, right)
                upd = mmf(panel, left)
                if lo > 0:
                    w[hi:, :lo] = w[hi:, :lo] - upd[:, :lo]
                w[hi:, lo:hi] = -upd[:, lo:]


def gate_terms(coupling):
    hopping = coupling[0]
    ising_term = coupling[1]
    field_term = coupling[2]
    rotation = 0.5 * tau_step * hopping
    middle_scale = jnp.exp(0.25 * tau_step * ising_term)
    weight_empty = jnp.exp(-tau_step * (0.25 * ising_term - 0.5 * field_term))
    weight_full = jnp.exp(-tau_step * (0.25 * ising_term + 0.5 * field_term))
    weight_stay = middle_scale * jnp.cosh(rotation)
    weight_swap = -middle_scale * jnp.sinh(rotation)
    return jnp.stack([weight_empty, weight_stay, weight_swap, weight_full])


def update_sectors(left, top, low, bdims, sketch_t, ranks, weights, outs, scratch):
    basis_refs, coef_refs, norm_ref = outs
    two_ref, sample_ref, tri_refs = scratch
    w_empty, w_stay, w_swap, w_full = (weights[i] for i in range(4))
    size = sample_ref.shape[1]

    def product(x, y):
        return mm(x, y, bdims).astype(jnp.bfloat16).astype(jnp.float32)

    up_stay = product(left(0, 1), top(0))
    stay_up = product(left(0, 0), low(0))
    for i in range(2):
        up_up = product(left(i, 1), low(i + 1))
        two_ref[i, size:, :size] = (w_swap * stay_up + w_stay * up_stay).astype(jnp.bfloat16)
        two_ref[i, size:, size:] = (w_full * up_up).astype(jnp.bfloat16)
        stay_stay = product(left(i + 1, 0), top(i))
        stay_up = product(left(i + 1, 0), low(i + 1))
        up_stay = product(left(i + 1, 1), top(i + 1))
        two_ref[i, :size, :size] = (w_empty * stay_stay).astype(jnp.bfloat16)
        two_ref[i, :size, size:] = (w_stay * stay_up + w_swap * up_stay).astype(jnp.bfloat16)
    row = lax.broadcasted_iota(jnp.int32, (size, size), 0)
    column = lax.broadcasted_iota(jnp.int32, (size, size), 1)
    row_wide = lax.broadcasted_iota(jnp.int32, (size, 2 * size), 0)
    for i in range(2):
        sample = mm(sketch_t[...], two_ref[i], NT)
        sample = jnp.where(row_wide < ranks[i], sample, 0.0)
        sample_ref[i] = sample
        high, low_part = split(sample)
        cross = mm(high, low_part, NT)
        gram = mm(high, high, NT) + (cross + cross.T)
        tri_refs[i][...] = gram + jnp.where((row == column) & (row >= ranks[i]), 1.0, 0.0)
    inv_cholesky(tri_refs)
    total = jnp.zeros((1, 1), jnp.float32)
    for i in range(2):
        basis = mm3(tri_refs[i][...], sample_ref[i]) * math.sqrt(size)
        basis = basis.astype(jnp.bfloat16)
        basis_refs[i][...] = basis
        coef = mm(basis, two_ref[i])
        total = total + jnp.sum(jnp.sum(coef * coef, axis=1, keepdims=True), axis=0, keepdims=True)
        coef_refs[i][...] = coef.astype(jnp.bfloat16)
    norm_ref[...] = jnp.broadcast_to(total, norm_ref.shape)


def first_kernel(side, ranks, weights, own, other, outer, lower, sketch_t, *refs):
    outs, (left_ref, top_ref, low_ref), scratch = refs[:5], refs[5:8], refs[8:]

    @pl.when(side[0] == 0)
    def _():
        left_ref[0] = outer[...]
        left_ref[1] = own[0]
        left_ref[2] = own[1]
        low_ref[0] = lower[...]
        for i in range(3):
            top_ref[i] = other[i, 0]
        for i in range(2):
            low_ref[i + 1] = other[i, 1]

    @pl.when(side[0] == 1)
    def _():
        for i in range(3):
            left_ref[i] = other[i]
            low_ref[i] = own[i + 1, 1]
        for i in range(2):
            top_ref[i] = own[i + 2, 0]
        top_ref[2] = outer[0]

    update_sectors(
        lambda k, s: left_ref[k, s],
        lambda k: top_ref[k],
        lambda k: low_ref[k],
        NN,
        sketch_t,
        ranks,
        weights,
        (outs[:2], outs[2:4], outs[4]),
        (scratch[0], scratch[1], scratch[2:4]),
    )


def second_kernel(ranks, weights, coef_outer, coef_a, coef_b, basis_a, basis_b, basis_outer, sketch_t, *refs):
    outs, scratch = refs[:5], refs[5:]
    size = basis_a.shape[0]
    coefs = (coef_outer, coef_a, coef_b)
    bases = (basis_a, basis_b, basis_outer)
    update_sectors(
        lambda k, s: coefs[k][:, s * size : (s + 1) * size],
        lambda k: bases[k][:, :size],
        lambda k: bases[k][:, size:],
        NT,
        sketch_t,
        ranks,
        weights,
        (outs[:2], outs[2:4], outs[4]),
        (scratch[0], scratch[1], scratch[2:4]),
    )


def last_kernel(side, scale, coef_a, coef_b, coef_c, coef_d, own_a, own_b, sib_a, sib_b, outer, out):
    size = outer.shape[0]

    @pl.when(side[0] == 0)
    def _():
        for i, coef in enumerate((coef_a, coef_b, coef_c, coef_d)):
            scaled = (coef[...].astype(jnp.float32) * scale[0]).astype(jnp.bfloat16)
            out[0, i, 0] = scaled[:, :size]
            out[0, i, 1] = scaled[:, size:]

    @pl.when(side[0] == 1)
    def _():
        def flip(block):
            return block.astype(jnp.float32).T.astype(jnp.bfloat16)

        bases = (sib_a, sib_b, own_a, own_b)
        for i, basis in enumerate(bases):
            out[0, i, 0] = flip(basis[:, :size])
            if i > 0:
                out[0, i - 1, 1] = flip(basis[:, size:])
        out[0, 3, 1] = flip(outer[...])


VMEM = pl.BlockSpec(memory_space=pltpu.VMEM)
SMEM = pl.BlockSpec(memory_space=pltpu.SMEM)


def update_call(kernel, scalars, arrays, gather, name):
    size = arrays[-1].shape[0]
    block = jax.ShapeDtypeStruct((size, 2 * size), jnp.bfloat16)
    bf16 = jnp.bfloat16
    extra = [
        pltpu.VMEM((3, 2, size, size), bf16),
        pltpu.VMEM((3, size, size), bf16),
        pltpu.VMEM((3, size, size), bf16),
    ]
    return pl.pallas_call(
        kernel,
        out_shape=[block] * 4 + [jax.ShapeDtypeStruct((8, 128), jnp.float32)],
        in_specs=[SMEM] * len(scalars) + [VMEM] * len(arrays),
        out_specs=[VMEM] * 5,
        scratch_shapes=(extra if gather else [])
        + [
            pltpu.VMEM((2, 2 * size, 2 * size), bf16),
            pltpu.VMEM((2, size, 2 * size), jnp.float32),
            pltpu.VMEM((size, size), jnp.float32),
            pltpu.VMEM((size, size), jnp.float32),
        ],
        cost_estimate=pl.CostEstimate(flops=4 * 10**9, bytes_accessed=4 * 10**6, transcendentals=0),
        name=name,
    )(*scalars, *arrays)


def local_mask(site_block, sizes_row, first_sector):
    sector_count = site_block.shape[0]
    block_width = site_block.shape[-1]
    right_ext = jnp.concatenate([sizes_row[1], jnp.zeros((1,), jnp.int32)])
    left_here = lax.dynamic_slice_in_dim(sizes_row[0], first_sector, sector_count)
    right_here = lax.dynamic_slice_in_dim(right_ext, first_sector, sector_count)
    right_next = lax.dynamic_slice_in_dim(right_ext, first_sector + 1, sector_count)
    row_index = jnp.arange(block_width, dtype=jnp.int32)
    row_keep = row_index[None, :] < left_here[:, None]
    col_stay = row_index[None, :] < right_here[:, None]
    col_next = row_index[None, :] < right_next[:, None]
    keep_zero = row_keep[:, :, None] & col_stay[:, None, :]
    keep_one = row_keep[:, :, None] & col_next[:, None, :]
    keep_both = jnp.stack([keep_zero, keep_one], axis=1)
    return jnp.where(keep_both, site_block, jnp.zeros_like(site_block))


def body(sites, blocks, site_tensors, sketch, bond_sizes, kept_ranks, couplings):
    sector_count = site_tensors.shape[1]
    half = sector_count // 2
    size = site_tensors.shape[-1]
    chain = lax.axis_index("chain")
    block = lax.axis_index("block")
    side = lax.rem(chain, 2)
    is_left = side == 0
    first_sector = block * sector_count
    own_first = first_sector + half * side

    def send(value, route):
        pairs = []
        for c in range(sites):
            for b in range(blocks):
                for tc, tb in route(c, b):
                    if 0 <= tb < blocks:
                        pairs.append((c * blocks + b, (tc % sites) * blocks + tb))
        return lax.ppermute(value, ("chain", "block"), pairs)

    def sibling(c, b):
        return [(c ^ 1, b)]

    def only(parity, dc, db):
        return lambda c, b: [(c + dc, b + db)] if c % 2 == parity else []

    def both(even_step, odd_step):
        return lambda c, b: [(c + (even_step, odd_step)[c % 2][0], b + (even_step, odd_step)[c % 2][1])]

    bond_row = jnp.concatenate([kept_ranks[0, 1].astype(jnp.float32), couplings[0, 1]])
    from_odd = send(bond_row, only(1, -1, 0))
    bond_row = jnp.where(is_left, from_odd, bond_row)

    own = local_mask(site_tensors[0], bond_sizes[0], first_sector)
    wanted = lax.dynamic_slice_in_dim(own, 1 - side, 3)
    other = send(wanted, sibling)
    outer = send(jnp.where(is_left, own[3], own[0]), both((0, 1), (0, -1)))
    lower = send(own[3, 1], only(1, -1, 1))

    even_ranks = jnp.where(is_left, kept_ranks[0, 1], kept_ranks[0, 0])
    even_ranks = lax.dynamic_slice_in_dim(even_ranks, own_first, half)
    even_weights = gate_terms(jnp.where(is_left, couplings[0, 1], couplings[0, 0]))
    odd_ranks = lax.dynamic_slice_in_dim(bond_row[:-3].astype(jnp.int32), own_first, half)
    odd_weights = gate_terms(bond_row[-3:])
    sketch_t = sketch.T
    side_row = side.reshape(1)
    target = float(sector_count * blocks * size * size)

    basis_a, basis_b, coef_a, coef_b, part = update_call(
        first_kernel,
        (side_row, even_ranks, even_weights),
        (own, other, outer, lower, sketch_t),
        True,
        "even_update",
    )
    far_a = send(basis_a, lambda c, b: [(c - 2, b)])
    far_b = send(basis_b, lambda c, b: [(c - 2, b)])
    coef_outer = send(coef_b, both((1, 0), (-1, 1)))
    far_outer = send(far_a, both((1, -1), (-1, 0)))
    part = part[0, :1]
    even_norm = lax.psum(part + send(part, sibling), "block")[0]
    odd_weights = odd_weights * jnp.sqrt(target / even_norm)

    basis_a, basis_b, coef_a, coef_b, part = update_call(
        second_kernel,
        (odd_ranks, odd_weights),
        (coef_outer, coef_a, coef_b, far_a, far_b, far_outer, sketch_t),
        False,
        "odd_update",
    )
    to_even = only(0, 2, 0)
    to_odd = only(1, 1, 0)
    new_a = send(coef_a, to_even)
    new_c = send(coef_a, to_odd)
    new_b = send(coef_b, to_even)
    new_d = send(coef_b, to_odd)
    sib_a = send(basis_a, only(0, 1, 0))
    sib_b = send(basis_b, only(0, 1, 0))
    basis_outer = send(basis_a[:, size:], only(0, 1, -1))
    part = part[0, :1]
    odd_norm = lax.psum(send(part, to_even) + send(part, to_odd), "block")
    scale = jnp.sqrt(target / odd_norm)
    return pl.pallas_call(
        last_kernel,
        out_shape=jax.ShapeDtypeStruct(site_tensors.shape, jnp.bfloat16),
        in_specs=[SMEM] * 2 + [VMEM] * 9,
        out_specs=VMEM,
        name="assemble",
    )(side_row, scale, new_a, new_b, new_c, new_d, basis_a, basis_b, sib_a, sib_b, basis_outer)


def solution(mesh):
    placed = (
        P("chain", "block", None, None, None),
        P(),
        P("chain", None, None),
        P("chain", None, None),
        P("chain", None, None),
    )
    return jax.shard_map(
        functools.partial(body, mesh.shape["chain"], mesh.shape["block"]),
        mesh=mesh,
        in_specs=placed,
        out_specs=P("chain", "block", None, None, None),
        check_vma=False,
    )
```

```python
import functools
import math

import jax
import jax.numpy as jnp
from jax import lax
from jax.experimental import pallas as pl
from jax.experimental.pallas import tpu as pltpu
from jax.sharding import PartitionSpec as P

tau_step = 0.5
NN = (((1,), (0,)), ((), ()))
NT = (((1,), (1,)), ((), ()))


def mm(x, y, dims=NN):
    return lax.dot_general(x, y, dims, preferred_element_type=jnp.float32)


def split(x):
    high = x.astype(jnp.bfloat16)
    low = (x - high.astype(jnp.float32)).astype(jnp.bfloat16)
    return high, low


def mm3(x, y, dims=NN):
    x_high, x_low = split(x)
    y_high, y_low = split(y)
    return mm(x_high, y_high, dims) + (mm(x_high, y_low, dims) + mm(x_low, y_high, dims))


def inv_factors(blocks):
    nb = blocks[0].shape[0]
    ngr = nb // 8
    eye = (lax.broadcasted_iota(jnp.int32, (nb, nb), 0) == lax.broadcasted_iota(jnp.int32, (nb, nb), 1)).astype(jnp.float32)
    work = []
    for g in blocks:
        full = jnp.concatenate([g, eye], axis=1)
        work.append([full[8 * i: 8 * i + 8, :] for i in range(ngr)])
    lane = lax.broadcasted_iota(jnp.int32, (8, 2 * nb), 1)
    sub = lax.broadcasted_iota(jnp.int32, (8, 2 * nb), 0)
    for j in range(nb):
        gj, sj = j // 8, j % 8
        for w in work:
            row = w[gj][sj: sj + 1, :]
            piv = row[:, j: j + 1]
            t = row * (1.0 / piv)
            tb = jnp.broadcast_to(t, (8, 2 * nb))
            for i in range(gj, ngr):
                if i == gj and sj == 7:
                    continue
                c = jnp.broadcast_to(w[i][:, j: j + 1], (8, 2 * nb))
                if i == gj:
                    c = jnp.where(sub > sj, c, 0.0)
                w[i] = w[i] - c * tb
    out = []
    for w in work:
        rows = []
        for i in range(ngr):
            d = jnp.sum(jnp.where(lane == sub + 8 * i, w[i], 0.0), axis=1, keepdims=True)
            rows.append(w[i] * lax.rsqrt(d))
        full = jnp.concatenate(rows, axis=0)
        out.append(full[:, nb:])
    return out

def inv_cholesky(w_refs, nb=64, mmf=mm3):
    n = w_refs[0].shape[-1]
    for k in range(n // nb):
        lo, hi = k * nb, (k + 1) * nb
        xs = inv_factors([w[lo:hi, lo:hi] for w in w_refs])
        for w, x in zip(w_refs, xs):
            if hi < n:
                panel = mmf(w[hi:, lo:hi], x, NT)
                right = mmf(x, w[lo:hi, hi:])
            if lo > 0:
                left = jnp.concatenate([mmf(x, w[lo:hi, :lo]), x], axis=1)
            else:
                left = x
            w[lo:hi, :hi] = left
            if hi < n:
                w[lo:hi, hi:] = jnp.zeros((nb, n - hi), jnp.float32)
                w[hi:, hi:] = w[hi:, hi:] - mmf(panel, right)
                upd = mmf(panel, left)
                if lo > 0:
                    w[hi:, :lo] = w[hi:, :lo] - upd[:, :lo]
                w[hi:, lo:hi] = -upd[:, lo:]


MESH = pl.DeviceIdType.MESH
VMEM = pl.BlockSpec(memory_space=pltpu.VMEM)


def gate_terms(coupling):
    hopping = coupling[0]
    ising_term = coupling[1]
    field_term = coupling[2]
    rotation = 0.5 * tau_step * hopping
    middle_scale = jnp.exp(0.25 * tau_step * ising_term)
    weight_empty = jnp.exp(-tau_step * (0.25 * ising_term - 0.5 * field_term))
    weight_full = jnp.exp(-tau_step * (0.25 * ising_term + 0.5 * field_term))
    weight_stay = middle_scale * jnp.cosh(rotation)
    weight_swap = -middle_scale * jnp.sinh(rotation)
    return jnp.stack([weight_empty, weight_stay, weight_swap, weight_full])


def update_sectors(left, top, low, bdims, sketch_t, ranks, weights, basis_ref, coef_ref, part_ref, scratch, sent):
    two_ref, sample_ref, tri_refs = scratch
    w_empty, w_stay, w_swap, w_full = weights
    size = sample_ref.shape[1]

    def product(x, y):
        return mm(x, y, bdims).astype(jnp.bfloat16).astype(jnp.float32)

    up_stay = product(left(0, 1), top(0))
    stay_up = product(left(0, 0), low(0))
    for i in range(2):
        up_up = product(left(i, 1), low(i + 1))
        two_ref[i, size:, :size] = (w_swap * stay_up + w_stay * up_stay).astype(jnp.bfloat16)
        two_ref[i, size:, size:] = (w_full * up_up).astype(jnp.bfloat16)
        stay_stay = product(left(i + 1, 0), top(i))
        stay_up = product(left(i + 1, 0), low(i + 1))
        up_stay = product(left(i + 1, 1), top(i + 1))
        two_ref[i, :size, :size] = (w_empty * stay_stay).astype(jnp.bfloat16)
        two_ref[i, :size, size:] = (w_stay * stay_up + w_swap * up_stay).astype(jnp.bfloat16)
    row = lax.broadcasted_iota(jnp.int32, (size, size), 0)
    column = lax.broadcasted_iota(jnp.int32, (size, size), 1)
    row_wide = lax.broadcasted_iota(jnp.int32, (size, 2 * size), 0)
    for i in range(2):
        sample = mm(sketch_t[...], two_ref[i], NT)
        sample = jnp.where(row_wide.astype(jnp.float32) < ranks[i], sample, 0.0)
        sample_ref[i] = sample
        high, low_part = split(sample)
        cross = mm(high, low_part, NT)
        gram = mm(high, high, NT) + (cross + cross.T)
        free = (row == column) & (row.astype(jnp.float32) >= ranks[i])
        tri_refs[i][...] = gram + jnp.where(free, 1.0, 0.0)
    inv_cholesky(tri_refs)
    total = jnp.zeros((1, 1), jnp.float32)
    for i in range(2):
        basis = mm3(tri_refs[i][...], sample_ref[i]) * math.sqrt(size)
        basis_ref[i] = basis.astype(jnp.bfloat16)
    for i in range(2):
        coef = mm(basis_ref[i], two_ref[i])
        total = total + jnp.sum(jnp.sum(coef * coef, axis=1, keepdims=True), axis=0, keepdims=True)
        coef_ref[i] = coef.astype(jnp.bfloat16)
        sent(i)
    part_ref[...] = jnp.broadcast_to(total, part_ref.shape)


def signal_to(semaphore, chain, block):
    pl.semaphore_signal(semaphore, inc=1, device_id={"chain": chain, "block": block}, device_id_type=MESH)


def entry_kernel(blocks, own, row, other, outer, lower, sib_row, send_sems, recv_sems):
    chain = lax.axis_index("chain")
    block = lax.axis_index("block")
    side = lax.rem(chain, 2)
    sib = chain + 1 - 2 * side
    has_prev = block > 0
    has_next = block < blocks - 1
    even = side == 0
    odd = side == 1
    barrier = pltpu.get_barrier_semaphore()
    signal_to(barrier, sib, block)
    pl.when(has_next)(lambda: signal_to(barrier, chain, block + 1))
    pl.when(has_prev)(lambda: signal_to(barrier, chain, block - 1))
    pl.when(even & has_prev)(lambda: signal_to(barrier, sib, block - 1))
    pl.when(odd & has_next)(lambda: signal_to(barrier, sib, block + 1))
    prev_count = has_prev.astype(jnp.int32)
    next_count = has_next.astype(jnp.int32)
    pl.semaphore_wait(barrier, 1 + (2 - side) * prev_count + (1 + side) * next_count)

    def remote(src, dst, k, to_chain, to_block):
        return pltpu.make_async_remote_copy(
            src_ref=src,
            dst_ref=dst,
            send_sem=send_sems.at[k],
            recv_sem=recv_sems.at[k],
            device_id={"chain": to_chain, "block": to_block},
            device_id_type=MESH,
        )

    edge_next = remote(own.at[3], outer, 0, chain, block + 1)
    edge_prev = remote(own.at[0], outer, 0, chain, block - 1)
    edge_low = remote(own.at[3, 1], lower, 1, sib, block + 1)
    to_odd = remote(own.at[pl.ds(1, 3)], other, 2, sib, block)
    to_even = remote(own.at[pl.ds(0, 3)], other, 2, sib, block)
    rows = remote(row, sib_row, 3, sib, block)
    pl.when(even & has_next)(edge_next.start)
    pl.when(odd & has_prev)(edge_prev.start)
    pl.when(odd & has_next)(edge_low.start)
    rows.start()
    pl.when(even)(to_odd.start)
    pl.when(odd)(to_even.start)

    @pl.when((even & (block == 0)) | (odd & (block == blocks - 1)))
    def _():
        outer[...] = jnp.zeros_like(outer)

    @pl.when(odd | (block == 0))
    def _():
        lower[...] = jnp.zeros_like(lower)

    rows.wait()
    to_odd.wait()
    pl.when((even & has_prev) | (odd & has_next))(edge_next.wait_recv)
    pl.when((even & has_next) | (odd & has_prev))(edge_next.wait_send)
    pl.when(even & has_prev)(edge_low.wait_recv)
    pl.when(odd & has_next)(edge_low.wait_send)


def step_kernel(chips, blocks, target, even_row, odd_row, own, other, outer, lower, sketch_t, out, *refs):
    (left_ref, top_ref, low_ref, two_ref, sample_ref, tri_a, tri_b, basis_ref, coef_ref, far_ref, edge_ref) = refs[:11]
    (new_ref, sib_ref, bot_ref, part_ref, norm_ref, sum_ref, scale_ref, send_sems, recv_sems, nsend, nrecv) = refs[11:]
    size = bot_ref.shape[0]
    chain = lax.axis_index("chain")
    block = lax.axis_index("block")
    side = lax.rem(chain, 2)
    sib = chain + 1 - 2 * side
    sites = 2 * chips
    has_prev = block > 0
    has_next = block < blocks - 1
    even = side == 0
    odd = side == 1
    back = lax.rem(chain + sites - 2, sites)
    ahead = lax.rem(chain + 2, sites)
    ahead_even = lax.rem(chain + 2 - side, sites)
    back_odd = lax.rem(chain + sites - 1, sites)
    group = 2 * blocks
    me = side * blocks + block
    barrier = pltpu.get_barrier_semaphore()

    def peer(step):
        index = lax.rem(me + step, group)
        return index, chain - side + index // blocks, lax.rem(index, blocks)

    for step in range(1, group):
        _, to_chain, to_block = peer(step)
        signal_to(barrier, to_chain, to_block)
    signal_to(barrier, back, block)

    @pl.when(even)
    def _():
        signal_to(barrier, back_odd, block)
        signal_to(barrier, ahead, block)

    @pl.when(odd)
    def _():
        signal_to(barrier, ahead, block)
        signal_to(barrier, ahead_even, block)

    def remote(src, dst, k, to_chain, to_block):
        return pltpu.make_async_remote_copy(
            src_ref=src,
            dst_ref=dst,
            send_sem=send_sems.at[k],
            recv_sem=recv_sems.at[k],
            device_id={"chain": to_chain, "block": to_block},
            device_id_type=MESH,
        )

    def norm_copy(layer, step):
        index, to_chain, to_block = peer(step)
        return pltpu.make_async_remote_copy(
            src_ref=norm_ref.at[layer, me],
            dst_ref=norm_ref.at[layer, me],
            send_sem=nsend.at[layer, step],
            recv_sem=nrecv.at[layer, me],
            device_id={"chain": to_chain, "block": to_block},
            device_id_type=MESH,
        )

    def norm_arrival(layer, step):
        index, to_chain, to_block = peer(step)
        return pltpu.make_async_remote_copy(
            src_ref=norm_ref.at[layer, index],
            dst_ref=norm_ref.at[layer, index],
            send_sem=nsend.at[layer, step],
            recv_sem=nrecv.at[layer, index],
            device_id={"chain": to_chain, "block": to_block},
            device_id_type=MESH,
        )

    def share_norm(layer):
        norm_ref[layer, me] = part_ref[...]
        for step in range(1, group):
            norm_copy(layer, step).start()

    def norm_scale(layer):
        for step in range(1, group):
            norm_arrival(layer, step).wait_recv()
        total = norm_ref[layer, 0]
        for i in range(1, group):
            total = total + norm_ref[layer, i]
        return jnp.sqrt(target / total)

    @pl.when(even)
    def _():
        left_ref[0] = outer[...]
        left_ref[1] = own[0]
        left_ref[2] = own[1]
        low_ref[0] = lower[...]
        for i in range(3):
            top_ref[i] = other[i, 0]
        for i in range(2):
            low_ref[i + 1] = other[i, 1]

    @pl.when(odd)
    def _():
        for i in range(3):
            left_ref[i] = other[i]
            low_ref[i] = own[i + 1, 1]
        for i in range(2):
            top_ref[i] = own[i + 2, 0]
        top_ref[2] = outer[0]

    @pl.when(even & (block == 0))
    def _():
        edge_ref[...] = jnp.zeros_like(edge_ref)

    @pl.when(odd & (block == blocks - 1))
    def _():
        far_ref[2] = jnp.zeros_like(far_ref[2])

    @pl.when(odd & (block == blocks - 1))
    def _():
        bot_ref[...] = jnp.zeros_like(bot_ref)

    def row_terms(ref):
        terms = [ref[0:1, i : i + 1] for i in range(8)]
        ranks = [jnp.where(even, terms[i], terms[i + 2]) for i in range(2)]
        return ranks, terms[4:]

    far = [remote(basis_ref.at[0, i], far_ref.at[i], i, back, block) for i in range(2)]
    edge_even = remote(coef_ref.at[0, 1], edge_ref, 2, sib, block)
    edge_odd = remote(coef_ref.at[0, 1], edge_ref, 2, sib, block + 1)
    pass_even = remote(far_ref.at[0], far_ref.at[2], 3, sib, block - 1)
    pass_odd = remote(far_ref.at[0], far_ref.at[2], 3, sib, block)

    def sent_even(i):
        if i == 0:
            pl.semaphore_wait(barrier, group + 2)
            far[0].start()
            far[1].start()
        else:
            pl.when(even)(edge_even.start)
            pl.when(odd & has_next)(edge_odd.start)

    scratch = (two_ref, sample_ref, (tri_a, tri_b))
    ranks, weights = row_terms(even_row)
    update_sectors(
        lambda k, s: left_ref[k, s],
        lambda k: top_ref[k],
        lambda k: low_ref[k],
        NN,
        sketch_t,
        ranks,
        weights,
        basis_ref.at[0],
        coef_ref.at[0],
        part_ref,
        scratch,
        sent_even,
    )
    share_norm(0)
    far[0].wait_recv()
    pl.when(even & has_prev)(pass_even.start)
    pl.when(odd)(pass_odd.start)
    scale = norm_scale(0)[0:1, 0:1]
    pl.when(odd | has_prev)(edge_even.wait_recv)
    far[1].wait_recv()
    pl.when(even | has_next)(pass_even.wait_recv)

    lefts = (edge_ref, coef_ref.at[0, 0], coef_ref.at[0, 1])
    ranks, weights = row_terms(odd_row)
    new_even = [remote(coef_ref.at[1, i], new_ref.at[i], 4 + i, ahead, block) for i in range(2)]
    new_odd = [remote(coef_ref.at[1, i], new_ref.at[2 + i], 6 + i, ahead_even, block) for i in range(2)]
    sibs = [remote(basis_ref.at[1, i], sib_ref.at[i], 8 + i, sib, block) for i in range(2)]
    bot = remote(basis_ref.at[1, 0, :, pl.ds(size, size)], bot_ref, 10, sib, block - 1)

    def sent_odd(i):
        pl.when(even)(new_even[i].start)
        pl.when(odd)(new_odd[i].start)
        pl.when(even)(sibs[i].start)
        if i == 1:
            pl.when(even & has_prev)(bot.start)

    update_sectors(
        lambda k, s: lefts[k][:, s * size : (s + 1) * size],
        lambda k: far_ref[k, :, :size],
        lambda k: far_ref[k, :, size:],
        NT,
        sketch_t,
        ranks,
        [w * scale for w in weights],
        basis_ref.at[1],
        coef_ref.at[1],
        part_ref,
        scratch,
        sent_odd,
    )
    share_norm(1)
    sum_ref[...] = norm_scale(1)
    scale_copy = remote(sum_ref, scale_ref, 11, ahead, block)
    pl.when(even)(scale_copy.start)

    @pl.when(even)
    def _():
        for i in range(2):
            new_even[i].wait_recv()
            new_odd[i].wait_recv()
        scale_copy.wait_recv()
        scale = scale_ref[0:1, 0:1]
        for i in range(4):
            scaled = (new_ref[i].astype(jnp.float32) * scale).astype(jnp.bfloat16)
            out[0, i, 0] = scaled[:, :size]
            out[0, i, 1] = scaled[:, size:]

    @pl.when(odd)
    def _():
        def flip(blocked):
            return blocked.astype(jnp.float32).T.astype(jnp.bfloat16)

        for i in range(2):
            sibs[i].wait_recv()
        pl.when(has_next)(bot.wait_recv)
        for i in range(4):
            basis = sib_ref[i] if i < 2 else basis_ref[1, i - 2]
            out[0, i, 0] = flip(basis[:, :size])
            if i > 0:
                out[0, i - 1, 1] = flip(basis[:, size:])
        out[0, 3, 1] = flip(bot_ref[...])

    for i in range(2):
        far[i].wait_send()
        pl.when(even)(new_even[i].wait_send)
        pl.when(odd)(new_odd[i].wait_send)
        pl.when(even)(sibs[i].wait_send)
    pl.when(even | has_next)(edge_even.wait_send)
    pl.when(odd | has_prev)(pass_even.wait_send)
    pl.when(even & has_prev)(bot.wait_send)
    pl.when(even)(scale_copy.wait_send)
    for layer in range(2):
        for step in range(1, group):
            norm_copy(layer, step).wait_send()


def local_mask(site_block, sizes_row, first_sector):
    sector_count = site_block.shape[0]
    block_width = site_block.shape[-1]
    right_ext = jnp.concatenate([sizes_row[1], jnp.zeros((1,), jnp.int32)])
    left_here = lax.dynamic_slice_in_dim(sizes_row[0], first_sector, sector_count)
    right_here = lax.dynamic_slice_in_dim(right_ext, first_sector, sector_count)
    right_next = lax.dynamic_slice_in_dim(right_ext, first_sector + 1, sector_count)
    row_index = jnp.arange(block_width, dtype=jnp.int32)
    row_keep = row_index[None, :] < left_here[:, None]
    col_stay = row_index[None, :] < right_here[:, None]
    col_next = row_index[None, :] < right_next[:, None]
    keep_zero = row_keep[:, :, None] & col_stay[:, None, :]
    keep_one = row_keep[:, :, None] & col_next[:, None, :]
    keep_both = jnp.stack([keep_zero, keep_one], axis=1)
    return jnp.where(keep_both, site_block, jnp.zeros_like(site_block))


def body(sites, blocks, site_tensors, sketch, bond_sizes, kept_ranks, couplings):
    sector_count = site_tensors.shape[1]
    size = site_tensors.shape[-1]
    bf16 = jnp.bfloat16
    f32 = jnp.float32
    chain = lax.axis_index("chain")
    block = lax.axis_index("block")
    is_left = lax.rem(chain, 2) == 0
    first_sector = block * sector_count

    counts = lax.dynamic_slice_in_dim(kept_ranks[0], first_sector, sector_count, axis=1).astype(f32)
    rows = jnp.concatenate([counts, gate_terms(couplings[0].T).T], axis=1)
    left_row, right_row = (jnp.broadcast_to(jnp.pad(rows[i], (0, 120))[None], (8, 128)) for i in range(2))
    own = local_mask(site_tensors[0], bond_sizes[0], first_sector)

    other, outer, lower, sib_row = pl.pallas_call(
        functools.partial(entry_kernel, blocks),
        out_shape=[
            jax.ShapeDtypeStruct((3, 2, size, size), bf16),
            jax.ShapeDtypeStruct((2, size, size), bf16),
            jax.ShapeDtypeStruct((size, size), bf16),
            jax.ShapeDtypeStruct((8, 128), f32),
        ],
        in_specs=[VMEM] * 2,
        out_specs=[VMEM] * 4,
        scratch_shapes=[pltpu.SemaphoreType.DMA((4,)), pltpu.SemaphoreType.DMA((4,))],
        compiler_params=pltpu.CompilerParams(collective_id=0, has_side_effects=True),
        name="entry",
    )(own, right_row)
    even_row = jnp.where(is_left, right_row, left_row)
    odd_row = jnp.where(is_left, sib_row, right_row)
    target = float(sector_count * blocks * size * size)
    group = 2 * blocks
    return pl.pallas_call(
        functools.partial(step_kernel, sites // 2, blocks, target),
        out_shape=jax.ShapeDtypeStruct(site_tensors.shape, bf16),
        in_specs=[VMEM] * 7,
        out_specs=VMEM,
        scratch_shapes=[
            pltpu.VMEM((3, 2, size, size), bf16),
            pltpu.VMEM((3, size, size), bf16),
            pltpu.VMEM((3, size, size), bf16),
            pltpu.VMEM((2, 2 * size, 2 * size), bf16),
            pltpu.VMEM((2, size, 2 * size), f32),
            pltpu.VMEM((size, size), f32),
            pltpu.VMEM((size, size), f32),
            pltpu.VMEM((2, 2, size, 2 * size), bf16),
            pltpu.VMEM((2, 2, size, 2 * size), bf16),
            pltpu.VMEM((3, size, 2 * size), bf16),
            pltpu.VMEM((size, 2 * size), bf16),
            pltpu.VMEM((4, size, 2 * size), bf16),
            pltpu.VMEM((2, size, 2 * size), bf16),
            pltpu.VMEM((size, size), bf16),
            pltpu.VMEM((8, 128), f32),
            pltpu.VMEM((2, group, 8, 128), f32),
            pltpu.VMEM((8, 128), f32),
            pltpu.VMEM((8, 128), f32),
            pltpu.SemaphoreType.DMA((12,)),
            pltpu.SemaphoreType.DMA((12,)),
            pltpu.SemaphoreType.DMA((2, group)),
            pltpu.SemaphoreType.DMA((2, group)),
        ],
        compiler_params=pltpu.CompilerParams(collective_id=1, has_side_effects=True),
        name="step",
    )(even_row, odd_row, own, other, outer, lower, sketch.T)


def solution(mesh):
    placed = (
        P("chain", "block", None, None, None),
        P(),
        P("chain", None, None),
        P("chain", None, None),
        P("chain", None, None),
    )
    return jax.shard_map(
        functools.partial(body, mesh.shape["chain"], mesh.shape["block"]),
        mesh=mesh,
        in_specs=placed,
        out_specs=P("chain", "block", None, None, None),
        check_vma=False,
    )
```

```python
import functools
import math

import jax
import jax.numpy as jnp
from jax import lax
from jax.experimental import pallas as pl
from jax.experimental.pallas import tpu as pltpu
from jax.sharding import PartitionSpec as P

tau_step = 0.5
NN = (((1,), (0,)), ((), ()))
NT = (((1,), (1,)), ((), ()))


def mm(x, y, dims=NN):
    return lax.dot_general(x, y, dims, preferred_element_type=jnp.float32)


def split(x):
    high = x.astype(jnp.bfloat16)
    low = (x - high.astype(jnp.float32)).astype(jnp.bfloat16)
    return high, low


def mm3(x, y, dims=NN):
    x_high, x_low = split(x)
    y_high, y_low = split(y)
    return mm(x_high, y_high, dims) + (mm(x_high, y_low, dims) + mm(x_low, y_high, dims))


def across(x):
    return jnp.broadcast_to(x, (8, 128))


def inv_factors(blocks):
    nb = blocks[0].shape[0]
    groups = nb // 8
    eye = lax.broadcasted_iota(jnp.int32, (nb, nb), 0) == lax.broadcasted_iota(jnp.int32, (nb, nb), 1)
    eye = eye.astype(jnp.float32)
    sub = lax.broadcasted_iota(jnp.int32, (8, 128), 0)
    one = jnp.ones((8, 128), jnp.float32)
    work = []
    for block in blocks:
        full = jnp.concatenate([block, eye], axis=1)
        work.append([full[8 * i : 8 * i + 8, :] for i in range(groups)])
    for g in range(groups):
        first = 8 * g
        states = []
        for w in work:
            cols = [across(w[g][:, first + p : first + p + 1]) for p in range(8)]
            states.append([w[g], w[g], cols, one, one])
        for p in range(8):
            for state in states:
                rows, solved, cols, pivots, inverses = state
                pivot = across(cols[p][p : p + 1, :])
                inverse = 1.0 / pivot
                factor = jnp.where(sub == p, 0.0, cols[p]) * inverse
                for q in range(p + 1, 8):
                    cols[q] = cols[q] - factor * across(cols[q][p : p + 1, :])
                state[0] = rows - jnp.where(sub > p, factor, 0.0) * across(rows[p : p + 1, :])
                state[1] = solved - factor * across(solved[p : p + 1, :])
                state[3] = jnp.where(sub == p, pivot, pivots)
                state[4] = jnp.where(sub == p, inverse, inverses)
        for w, (rows, solved, cols, pivots, inverses) in zip(work, states):
            w[g] = rows * lax.rsqrt(pivots)
            solved = solved * inverses
            spread = [across(solved[p : p + 1, :]) for p in range(8)]
            for i in range(g + 1, groups):
                terms = [across(w[i][:, first + p : first + p + 1]) * spread[p] for p in range(8)]
                terms = [terms[k] + terms[k + 1] for k in range(0, 8, 2)]
                w[i] = w[i] - ((terms[0] + terms[1]) + (terms[2] + terms[3]))
    return [jnp.concatenate(w, axis=0)[:, nb:] for w in work]


def inv_cholesky(w_refs, nb=64, mmf=mm3):
    n = w_refs[0].shape[-1]
    for k in range(n // nb):
        lo, hi = k * nb, (k + 1) * nb
        xs = inv_factors([w[lo:hi, lo:hi] for w in w_refs])
        for w, x in zip(w_refs, xs):
            if hi < n:
                panel = mmf(w[hi:, lo:hi], x, NT)
                right = mmf(x, w[lo:hi, hi:])
            if lo > 0:
                left = jnp.concatenate([mmf(x, w[lo:hi, :lo]), x], axis=1)
            else:
                left = x
            w[lo:hi, :hi] = left
            if hi < n:
                w[lo:hi, hi:] = jnp.zeros((nb, n - hi), jnp.float32)
                w[hi:, hi:] = w[hi:, hi:] - mmf(panel, right)
                upd = mmf(panel, left)
                if lo > 0:
                    w[hi:, :lo] = w[hi:, :lo] - upd[:, :lo]
                w[hi:, lo:hi] = -upd[:, lo:]


MESH = pl.DeviceIdType.MESH
VMEM = pl.BlockSpec(memory_space=pltpu.VMEM)


def update_sectors(left, top, low, bdims, sketch_t, ranks, weights, basis_ref, coef_ref, part_ref, scratch, sent):
    two_ref, sample_ref, tri_refs = scratch
    w_empty, w_stay, w_swap, w_full = weights
    size = sample_ref.shape[1]

    def product(x, y):
        return mm(x, y, bdims).astype(jnp.bfloat16).astype(jnp.float32)

    up_stay = product(left(0, 1), top(0))
    stay_up = product(left(0, 0), low(0))
    for i in range(2):
        up_up = product(left(i, 1), low(i + 1))
        two_ref[i, size:, :size] = (w_swap * stay_up + w_stay * up_stay).astype(jnp.bfloat16)
        two_ref[i, size:, size:] = (w_full * up_up).astype(jnp.bfloat16)
        stay_stay = product(left(i + 1, 0), top(i))
        stay_up = product(left(i + 1, 0), low(i + 1))
        up_stay = product(left(i + 1, 1), top(i + 1))
        two_ref[i, :size, :size] = (w_empty * stay_stay).astype(jnp.bfloat16)
        two_ref[i, :size, size:] = (w_stay * stay_up + w_swap * up_stay).astype(jnp.bfloat16)
    row = lax.broadcasted_iota(jnp.int32, (size, size), 0)
    column = lax.broadcasted_iota(jnp.int32, (size, size), 1)
    row_wide = lax.broadcasted_iota(jnp.int32, (size, 2 * size), 0)
    for i in range(2):
        sample = mm(sketch_t[...], two_ref[i], NT)
        sample = jnp.where(row_wide.astype(jnp.float32) < ranks[i], sample, 0.0)
        sample_ref[i] = sample
        high, low_part = split(sample)
        cross = mm(high, low_part, NT)
        gram = mm(high, high, NT) + (cross + cross.T)
        free = (row == column) & (row.astype(jnp.float32) >= ranks[i])
        tri_refs[i][...] = gram + jnp.where(free, 1.0, 0.0)
    inv_cholesky(tri_refs)
    total = jnp.zeros((1, 1), jnp.float32)
    for i in range(2):
        basis = mm3(tri_refs[i][...], sample_ref[i]) * math.sqrt(size)
        basis_ref[i] = basis.astype(jnp.bfloat16)
    for i in range(2):
        coef = mm(basis_ref[i], two_ref[i])
        total = total + jnp.sum(jnp.sum(coef * coef, axis=1, keepdims=True), axis=0, keepdims=True)
        coef_ref[i] = coef.astype(jnp.bfloat16)
        sent(i)
    part_ref[...] = jnp.broadcast_to(total, part_ref.shape)


def signal_to(semaphore, chain, block):
    pl.semaphore_signal(semaphore, inc=1, device_id={"chain": chain, "block": block}, device_id_type=MESH)


def entry_kernel(blocks, own, sketch, sizes, counts, terms, left, top, low, sketch_t, even_row, odd_row, *refs):
    (other, outer, lower, sib_sizes, sib_counts, sib_terms, send_sems, recv_sems) = refs
    size = outer.shape[-1]
    chain = lax.axis_index("chain")
    block = lax.axis_index("block")
    side = lax.rem(chain, 2)
    sib = chain + 1 - 2 * side
    first = block * own.shape[1] + side * 2
    has_prev = block > 0
    has_next = block < blocks - 1
    even = side == 0
    odd = side == 1
    barrier = pltpu.get_barrier_semaphore()
    signal_to(barrier, sib, block)
    pl.when(has_next)(lambda: signal_to(barrier, chain, block + 1))
    pl.when(has_prev)(lambda: signal_to(barrier, chain, block - 1))
    pl.when(even & has_prev)(lambda: signal_to(barrier, sib, block - 1))
    pl.when(odd & has_next)(lambda: signal_to(barrier, sib, block + 1))
    prev_count = has_prev.astype(jnp.int32)
    next_count = has_next.astype(jnp.int32)
    pl.semaphore_wait(barrier, 1 + (2 - side) * prev_count + (1 + side) * next_count)

    def remote(src, dst, k, to_chain, to_block):
        return pltpu.make_async_remote_copy(
            src_ref=src,
            dst_ref=dst,
            send_sem=send_sems.at[k],
            recv_sem=recv_sems.at[k],
            device_id={"chain": to_chain, "block": to_block},
            device_id_type=MESH,
        )

    edge_next = remote(own.at[0, 3], outer, 0, chain, block + 1)
    edge_prev = remote(own.at[0, 0, 0], outer.at[0], 1, chain, block - 1)
    edge_low = remote(own.at[0, 3, 1], lower, 2, sib, block + 1)
    to_odd = remote(own.at[0, pl.ds(1, 3)], other, 3, sib, block)
    to_even = remote(own.at[0, pl.ds(0, 3)], other, 3, sib, block)
    rows = [
        remote(sizes, sib_sizes, 4, sib, block),
        remote(counts, sib_counts, 5, sib, block),
        remote(terms, sib_terms, 6, sib, block),
    ]
    pl.when(even & has_next)(edge_next.start)
    pl.when(odd & has_next)(edge_low.start)
    pl.when(odd & has_prev)(edge_prev.start)
    for copy in rows:
        copy.start()
    pl.when(even)(to_odd.start)
    pl.when(odd)(to_even.start)

    @pl.when((even & (block == 0)) | (odd & (block == blocks - 1)))
    def _():
        outer[...] = jnp.zeros_like(outer)

    @pl.when(even & (block == 0))
    def _():
        lower[...] = jnp.zeros_like(lower)

    sketch_t[...] = sketch[...].astype(jnp.float32).T.astype(jnp.bfloat16)
    for copy in rows:
        copy.wait()

    def entry(row, index):
        lane = lax.broadcasted_iota(jnp.int32, row.shape, 1)
        return jnp.sum(jnp.where(lane == index, row.astype(jnp.float32), 0.0), axis=1, keepdims=True)

    def write_row(ref, count_row, term_row):
        hopping, ising, field = (term_row[:, i : i + 1] for i in range(3))
        rotation = 0.5 * tau_step * hopping
        middle = jnp.exp(0.25 * tau_step * ising)
        grow, shrink = jnp.exp(rotation), jnp.exp(-rotation)
        values = [
            entry(count_row, first),
            entry(count_row, first + 1),
            jnp.exp(-tau_step * (0.25 * ising - 0.5 * field)),
            middle * (0.5 * (grow + shrink)),
            -middle * (0.5 * (grow - shrink)),
            jnp.exp(-tau_step * (0.25 * ising + 0.5 * field)),
        ]
        lane = lax.broadcasted_iota(jnp.int32, ref.shape, 1)
        result = jnp.zeros(ref.shape, jnp.float32)
        for i, value in enumerate(values):
            result = jnp.where(lane == i, jnp.broadcast_to(value, ref.shape), result)
        ref[...] = result

    def pick(take, first_row, second_row):
        return jnp.where(take, first_row.astype(jnp.float32), second_row.astype(jnp.float32))

    write_row(
        even_row,
        pick(even, counts[0, 1:2, :], counts[0, 0:1, :]),
        pick(even, terms[0, 1:2, :], terms[0, 0:1, :]),
    )
    write_row(
        odd_row,
        pick(odd, counts[0, 1:2, :], sib_counts[0, 1:2, :]),
        pick(odd, terms[0, 1:2, :], sib_terms[0, 1:2, :]),
    )
    lefts = [pick(even, sizes[0, i : i + 1, :], sib_sizes[0, i : i + 1, :]) for i in range(2)]
    rights = [pick(odd, sizes[0, i : i + 1, :], sib_sizes[0, i : i + 1, :]) for i in range(2)]
    row = lax.broadcasted_iota(jnp.int32, (size, size), 0).astype(jnp.float32)
    column = lax.broadcasted_iota(jnp.int32, (size, size), 1).astype(jnp.float32)

    def cut(value, bond, sector, shift):
        keep = (row < entry(bond[0], sector)) & (column < entry(bond[1], sector + shift))
        return jnp.where(keep, value.astype(jnp.float32), 0.0).astype(jnp.bfloat16)

    def put_left(k, value):
        for s in range(2):
            left[k, s] = cut(value(s), lefts, first - 1 + k, s)

    def put_top(k, value):
        top[k] = cut(value, rights, first + k, 0)

    def put_low(k, value):
        low[k] = cut(value, rights, first - 1 + k, 1)

    @pl.when(even)
    def _():
        put_left(1, lambda s: own[0, 0, s])
        put_left(2, lambda s: own[0, 1, s])
        to_odd.wait()
        for i in range(3):
            put_top(i, other[i, 0])
        for i in range(2):
            put_low(i + 1, other[i, 1])
        pl.when(has_prev)(edge_next.wait_recv)
        pl.when(has_prev)(edge_low.wait_recv)
        put_left(0, lambda s: outer[s])
        put_low(0, lower[...])
        pl.when(has_next)(edge_next.wait_send)

    @pl.when(odd)
    def _():
        for i in range(3):
            put_low(i, own[0, i + 1, 1])
        for i in range(2):
            put_top(i, own[0, i + 2, 0])
        to_even.wait()
        for i in range(3):
            put_left(i, lambda s: other[i, s])
        pl.when(has_next)(edge_prev.wait_recv)
        put_top(2, outer[0])
        pl.when(has_prev)(edge_prev.wait_send)
        pl.when(has_next)(edge_low.wait_send)


def step_kernel(chips, blocks, target, left_ref, top_ref, low_ref, sketch_t, even_row, odd_row, out, *refs):
    (two_ref, sample_ref, tri_a, tri_b, basis_ref, coef_ref, far_ref, edge_ref) = refs[:8]
    (sib_ref, bot_ref, part_ref, norm_ref, sum_ref, scale_ref, send_sems, recv_sems, nsend, nrecv, turn) = refs[8:]
    size = bot_ref.shape[0]
    chain = lax.axis_index("chain")
    block = lax.axis_index("block")
    side = lax.rem(chain, 2)
    sib = chain + 1 - 2 * side
    sites = 2 * chips
    has_prev = block > 0
    has_next = block < blocks - 1
    even = side == 0
    odd = side == 1
    back = lax.rem(chain + sites - 2, sites)
    ahead = lax.rem(chain + 2, sites)
    ahead_even = lax.rem(chain + 2 - side, sites)
    back_odd = lax.rem(chain + sites - 1, sites)
    group = 2 * blocks
    me = side * blocks + block
    barrier = pltpu.get_barrier_semaphore()

    def peer(step):
        index = lax.rem(me + step, group)
        return index, chain - side + index // blocks, lax.rem(index, blocks)

    for step in range(1, group):
        _, to_chain, to_block = peer(step)
        signal_to(barrier, to_chain, to_block)
    signal_to(barrier, back, block)

    @pl.when(even)
    def _():
        signal_to(barrier, back_odd, block)
        signal_to(barrier, ahead, block)

    @pl.when(odd)
    def _():
        signal_to(barrier, ahead, block)
        signal_to(barrier, ahead_even, block)

    def remote(src, dst, k, to_chain, to_block):
        return pltpu.make_async_remote_copy(
            src_ref=src,
            dst_ref=dst,
            send_sem=send_sems.at[k],
            recv_sem=recv_sems.at[k],
            device_id={"chain": to_chain, "block": to_block},
            device_id_type=MESH,
        )

    def norm_copy(layer, step):
        index, to_chain, to_block = peer(step)
        return pltpu.make_async_remote_copy(
            src_ref=norm_ref.at[layer, me],
            dst_ref=norm_ref.at[layer, me],
            send_sem=nsend.at[layer, step],
            recv_sem=nrecv.at[layer, me],
            device_id={"chain": to_chain, "block": to_block},
            device_id_type=MESH,
        )

    def norm_arrival(layer, step):
        index, to_chain, to_block = peer(step)
        return pltpu.make_async_remote_copy(
            src_ref=norm_ref.at[layer, index],
            dst_ref=norm_ref.at[layer, index],
            send_sem=nsend.at[layer, step],
            recv_sem=nrecv.at[layer, index],
            device_id={"chain": to_chain, "block": to_block},
            device_id_type=MESH,
        )

    def share_norm(layer):
        norm_ref[layer, me] = part_ref[...]
        for step in range(1, group):
            norm_copy(layer, step).start()

    def norm_scale(layer):
        for step in range(1, group):
            norm_arrival(layer, step).wait_recv()
        total = norm_ref[layer, 0]
        for i in range(1, group):
            total = total + norm_ref[layer, i]
        return jnp.sqrt(target / total)

    @pl.when(even & (block == 0))
    def _():
        edge_ref[...] = jnp.zeros_like(edge_ref)

    @pl.when(odd & (block == blocks - 1))
    def _():
        far_ref[2] = jnp.zeros_like(far_ref[2])

    @pl.when(odd & (block == blocks - 1))
    def _():
        bot_ref[...] = jnp.zeros_like(bot_ref)

    def row_terms(ref):
        terms = [ref[0:1, i : i + 1] for i in range(6)]
        return terms[:2], terms[2:]

    far = [remote(basis_ref.at[0, i], far_ref.at[i], i, back, block) for i in range(2)]
    edge_even = remote(coef_ref.at[0, 1], edge_ref, 2, sib, block)
    edge_odd = remote(coef_ref.at[0, 1], edge_ref, 2, sib, block + 1)
    pass_even = remote(far_ref.at[0], far_ref.at[2], 3, sib, block - 1)
    pass_odd = remote(far_ref.at[0], far_ref.at[2], 3, sib, block)

    def sent_even(i):
        if i == 0:
            pl.semaphore_wait(barrier, group + 2)
            far[0].start()
            pl.when(even)(far[1].start)
        else:
            pl.when(even)(edge_even.start)
            pl.when(odd & has_next)(edge_odd.start)

    scratch = (two_ref, sample_ref, (tri_a, tri_b))
    ranks, weights = row_terms(even_row)
    update_sectors(
        lambda k, s: left_ref[k, s],
        lambda k: top_ref[k],
        lambda k: low_ref[k],
        NN,
        sketch_t,
        ranks,
        weights,
        basis_ref.at[0],
        coef_ref.at[0],
        part_ref,
        scratch,
        sent_even,
    )
    share_norm(0)
    far[0].wait_recv()
    pl.when(even & has_prev)(pass_even.start)
    pl.when(odd)(pass_odd.start)
    far[0].wait_send()

    @pl.when(even)
    def _():
        far[1].wait_send()
        signal_to(turn, sib, block)

    @pl.when(odd)
    def _():
        pl.semaphore_wait(turn, 1)
        far[1].start()

    scale = norm_scale(0)[0:1, 0:1]
    pl.when(odd | has_prev)(edge_even.wait_recv)
    far[1].wait_recv()
    pl.when(even | has_next)(pass_even.wait_recv)

    lefts = (edge_ref, coef_ref.at[0, 0], coef_ref.at[0, 1])
    ranks, weights = row_terms(odd_row)
    new_even, new_odd = [], []
    for i in range(2):
        for half in range(2):
            piece = coef_ref.at[1, i, :, pl.ds(half * size, size)]
            k = 2 * i + half
            new_even.append(remote(piece, out.at[0, i, half], 4 + k, ahead, block))
            new_odd.append(remote(piece, out.at[0, 2 + i, half], 8 + k, ahead_even, block))
    sibs = [remote(basis_ref.at[1, i], sib_ref.at[i], 12 + i, sib, block) for i in range(2)]
    bot = remote(basis_ref.at[1, 0, :, pl.ds(size, size)], bot_ref, 14, sib, block - 1)

    def sent_odd(i):
        for k in (2 * i, 2 * i + 1):
            pl.when(even)(new_even[k].start)
            pl.when(odd)(new_odd[k].start)
        pl.when(even)(sibs[i].start)
        if i == 1:
            pl.when(even & has_prev)(bot.start)

    update_sectors(
        lambda k, s: lefts[k][:, s * size : (s + 1) * size],
        lambda k: far_ref[k, :, :size],
        lambda k: far_ref[k, :, size:],
        NT,
        sketch_t,
        ranks,
        [w * scale for w in weights],
        basis_ref.at[1],
        coef_ref.at[1],
        part_ref,
        scratch,
        sent_odd,
    )
    share_norm(1)
    sum_ref[...] = norm_scale(1)
    scale_copy = remote(sum_ref, scale_ref, 15, ahead, block)
    pl.when(even)(scale_copy.start)

    @pl.when(even)
    def _():
        for k in range(4):
            new_even[k].wait_recv()
            new_odd[k].wait_recv()
        scale_copy.wait_recv()
        scale = scale_ref[0:1, 0:1]
        for i in range(4):
            for half in range(2):
                out[0, i, half] = (out[0, i, half].astype(jnp.float32) * scale).astype(jnp.bfloat16)

    @pl.when(odd)
    def _():
        def flip(blocked):
            return blocked.astype(jnp.float32).T.astype(jnp.bfloat16)

        for i in range(2):
            sibs[i].wait_recv()
        pl.when(has_next)(bot.wait_recv)
        for i in range(4):
            basis = sib_ref[i] if i < 2 else basis_ref[1, i - 2]
            out[0, i, 0] = flip(basis[:, :size])
            if i > 0:
                out[0, i - 1, 1] = flip(basis[:, size:])
        out[0, 3, 1] = flip(bot_ref[...])

    pl.when(odd)(far[1].wait_send)
    for k in range(4):
        pl.when(even)(new_even[k].wait_send)
        pl.when(odd)(new_odd[k].wait_send)
    for i in range(2):
        pl.when(even)(sibs[i].wait_send)
    pl.when(even | has_next)(edge_even.wait_send)
    pl.when(odd | has_prev)(pass_even.wait_send)
    pl.when(even & has_prev)(bot.wait_send)
    pl.when(even)(scale_copy.wait_send)
    for layer in range(2):
        for step in range(1, group):
            norm_copy(layer, step).wait_send()


def body(sites, blocks, site_tensors, sketch, bond_sizes, kept_ranks, couplings):
    sector_count = site_tensors.shape[1]
    size = site_tensors.shape[-1]
    bf16 = jnp.bfloat16
    f32 = jnp.float32
    row = jax.ShapeDtypeStruct((8, 128), f32)
    terms = pl.pallas_call(
        functools.partial(entry_kernel, blocks),
        out_shape=[
            jax.ShapeDtypeStruct((3, 2, size, size), bf16),
            jax.ShapeDtypeStruct((3, size, size), bf16),
            jax.ShapeDtypeStruct((3, size, size), bf16),
            jax.ShapeDtypeStruct((size, 2 * size), bf16),
            row,
            row,
        ],
        in_specs=[VMEM] * 5,
        out_specs=[VMEM] * 6,
        scratch_shapes=[
            pltpu.VMEM((3, 2, size, size), bf16),
            pltpu.VMEM((2, size, size), bf16),
            pltpu.VMEM((size, size), bf16),
            pltpu.VMEM(bond_sizes.shape, jnp.int32),
            pltpu.VMEM(kept_ranks.shape, jnp.int32),
            pltpu.VMEM(couplings.shape, f32),
            pltpu.SemaphoreType.DMA((7,)),
            pltpu.SemaphoreType.DMA((7,)),
        ],
        compiler_params=pltpu.CompilerParams(collective_id=0, has_side_effects=True),
        name="entry",
    )(site_tensors, sketch, bond_sizes, kept_ranks, couplings)
    target = float(sector_count * blocks * size * size)
    group = 2 * blocks
    return pl.pallas_call(
        functools.partial(step_kernel, sites // 2, blocks, target),
        out_shape=jax.ShapeDtypeStruct(site_tensors.shape, bf16),
        in_specs=[VMEM] * 6,
        out_specs=VMEM,
        scratch_shapes=[
            pltpu.VMEM((2, 2 * size, 2 * size), bf16),
            pltpu.VMEM((2, size, 2 * size), f32),
            pltpu.VMEM((size, size), f32),
            pltpu.VMEM((size, size), f32),
            pltpu.VMEM((2, 2, size, 2 * size), bf16),
            pltpu.VMEM((2, 2, size, 2 * size), bf16),
            pltpu.VMEM((3, size, 2 * size), bf16),
            pltpu.VMEM((size, 2 * size), bf16),
            pltpu.VMEM((2, size, 2 * size), bf16),
            pltpu.VMEM((size, size), bf16),
            pltpu.VMEM((8, 128), f32),
            pltpu.VMEM((2, group, 8, 128), f32),
            pltpu.VMEM((8, 128), f32),
            pltpu.VMEM((8, 128), f32),
            pltpu.SemaphoreType.DMA((16,)),
            pltpu.SemaphoreType.DMA((16,)),
            pltpu.SemaphoreType.DMA((2, group)),
            pltpu.SemaphoreType.DMA((2, group)),
            pltpu.SemaphoreType.REGULAR,
        ],
        compiler_params=pltpu.CompilerParams(collective_id=1, has_side_effects=True),
        name="step",
    )(*terms)


def solution(mesh):
    placed = (
        P("chain", "block", None, None, None),
        P(),
        P("chain", None, None),
        P("chain", None, None),
        P("chain", None, None),
    )
    return jax.shard_map(
        functools.partial(body, mesh.shape["chain"], mesh.shape["block"]),
        mesh=mesh,
        in_specs=placed,
        out_specs=P("chain", "block", None, None, None),
        check_vma=False,
    )
```

```python
import functools
import math

import jax
import jax.numpy as jnp
from jax import lax
from jax.experimental import pallas as pl
from jax.experimental.pallas import tpu as pltpu
from jax.sharding import PartitionSpec as P

tau_step = 0.5
NN = (((1,), (0,)), ((), ()))
NT = (((1,), (1,)), ((), ()))


def mm(x, y, dims=NN):
    return lax.dot_general(x, y, dims, preferred_element_type=jnp.float32)


def split(x):
    high = x.astype(jnp.bfloat16)
    low = (x - high.astype(jnp.float32)).astype(jnp.bfloat16)
    return high, low


def mm3(x, y, dims=NN):
    x_high, x_low = split(x)
    y_high, y_low = split(y)
    return mm(x_high, y_high, dims) + (mm(x_high, y_low, dims) + mm(x_low, y_high, dims))


def across(x):
    return jnp.broadcast_to(x, (8, 128))


def inv_factors(blocks):
    nb = blocks[0].shape[0]
    groups = nb // 8
    eye = lax.broadcasted_iota(jnp.int32, (nb, nb), 0) == lax.broadcasted_iota(jnp.int32, (nb, nb), 1)
    eye = eye.astype(jnp.float32)
    sub = lax.broadcasted_iota(jnp.int32, (8, 128), 0)
    one = jnp.ones((8, 128), jnp.float32)
    work = []
    for block in blocks:
        full = jnp.concatenate([block, eye], axis=1)
        work.append([full[8 * i : 8 * i + 8, :] for i in range(groups)])
    for g in range(groups):
        first = 8 * g
        states = []
        for w in work:
            cols = [across(w[g][:, first + p : first + p + 1]) for p in range(8)]
            states.append([w[g], w[g], cols, one, one])
        for p in range(8):
            for state in states:
                rows, solved, cols, pivots, inverses = state
                pivot = across(cols[p][p : p + 1, :])
                inverse = 1.0 / pivot
                factor = jnp.where(sub == p, 0.0, cols[p]) * inverse
                for q in range(p + 1, 8):
                    cols[q] = cols[q] - factor * across(cols[q][p : p + 1, :])
                state[0] = rows - jnp.where(sub > p, factor, 0.0) * across(rows[p : p + 1, :])
                state[1] = solved - factor * across(solved[p : p + 1, :])
                state[3] = jnp.where(sub == p, pivot, pivots)
                state[4] = jnp.where(sub == p, inverse, inverses)
        for w, (rows, solved, cols, pivots, inverses) in zip(work, states):
            w[g] = rows * lax.rsqrt(pivots)
            solved = solved * inverses
            spread = [across(solved[p : p + 1, :]) for p in range(8)]
            for i in range(g + 1, groups):
                terms = [across(w[i][:, first + p : first + p + 1]) * spread[p] for p in range(8)]
                terms = [terms[k] + terms[k + 1] for k in range(0, 8, 2)]
                w[i] = w[i] - ((terms[0] + terms[1]) + (terms[2] + terms[3]))
    return [jnp.concatenate(w, axis=0)[:, nb:] for w in work]


def inv_cholesky(w_refs, nb=64, mmf=mm3):
    n = w_refs[0].shape[-1]
    for k in range(n // nb):
        lo, hi = k * nb, (k + 1) * nb
        xs = inv_factors([w[lo:hi, lo:hi] for w in w_refs])
        for w, x in zip(w_refs, xs):
            if hi < n:
                panel = mmf(w[hi:, lo:hi], x, NT)
                right = mmf(x, w[lo:hi, hi:])
            if lo > 0:
                left = jnp.concatenate([mmf(x, w[lo:hi, :lo]), x], axis=1)
            else:
                left = x
            w[lo:hi, :hi] = left
            if hi < n:
                w[lo:hi, hi:] = jnp.zeros((nb, n - hi), jnp.float32)
                w[hi:, hi:] = w[hi:, hi:] - mmf(panel, right)
                upd = mmf(panel, left)
                if lo > 0:
                    w[hi:, :lo] = w[hi:, :lo] - upd[:, :lo]
                w[hi:, lo:hi] = -upd[:, lo:]


MESH = pl.DeviceIdType.MESH
VMEM = pl.BlockSpec(memory_space=pltpu.VMEM)


def update_sectors(left, top, low, bdims, sketch_t, ranks, weights, basis_ref, coef_ref, part_ref, scratch, before, sent):
    two_ref, sample_ref, tri_refs = scratch
    w_empty, w_stay, w_swap, w_full = weights
    size = sample_ref.shape[1]

    def product(x, y):
        return mm(x, y, bdims).astype(jnp.bfloat16).astype(jnp.float32)

    row = lax.broadcasted_iota(jnp.int32, (size, size), 0)
    column = lax.broadcasted_iota(jnp.int32, (size, size), 1)
    row_wide = lax.broadcasted_iota(jnp.int32, (size, 2 * size), 0)
    total = jnp.zeros((1, 1), jnp.float32)
    for i in range(2):
        before(i)
        if i == 0:
            up_stay = product(left(0, 1), top(0))
            stay_up = product(left(0, 0), low(0))
        up_up = product(left(i, 1), low(i + 1))
        two_ref[i, size:, :size] = (w_swap * stay_up + w_stay * up_stay).astype(jnp.bfloat16)
        two_ref[i, size:, size:] = (w_full * up_up).astype(jnp.bfloat16)
        stay_stay = product(left(i + 1, 0), top(i))
        stay_up = product(left(i + 1, 0), low(i + 1))
        up_stay = product(left(i + 1, 1), top(i + 1))
        two_ref[i, :size, :size] = (w_empty * stay_stay).astype(jnp.bfloat16)
        two_ref[i, :size, size:] = (w_stay * stay_up + w_swap * up_stay).astype(jnp.bfloat16)
        sample = mm(sketch_t[...], two_ref[i], NT)
        sample = jnp.where(row_wide.astype(jnp.float32) < ranks[i], sample, 0.0)
        sample_ref[i] = sample
        high, low_part = split(sample)
        cross = mm(high, low_part, NT)
        gram = mm(high, high, NT) + (cross + cross.T)
        free = (row == column) & (row.astype(jnp.float32) >= ranks[i])
        tri_refs[i][...] = gram + jnp.where(free, 1.0, 0.0)
        inv_cholesky(tri_refs[i : i + 1])
        basis = mm3(tri_refs[i][...], sample_ref[i]) * math.sqrt(size)
        basis_ref[i] = basis.astype(jnp.bfloat16)
        coef = mm(basis_ref[i], two_ref[i])
        total = total + jnp.sum(jnp.sum(coef * coef, axis=1, keepdims=True), axis=0, keepdims=True)
        coef_ref[i] = coef.astype(jnp.bfloat16)
        sent(i)
    part_ref[...] = jnp.broadcast_to(total, part_ref.shape)


def signal_to(semaphore, chain, block):
    pl.semaphore_signal(semaphore, inc=1, device_id={"chain": chain, "block": block}, device_id_type=MESH)


def entry_kernel(blocks, own, sketch, sizes, counts, terms, left, top, low, sketch_t, even_row, odd_row, *refs):
    (other, outer, lower, sib_sizes, sib_counts, sib_terms, send_sems, recv_sems) = refs
    size = outer.shape[-1]
    chain = lax.axis_index("chain")
    block = lax.axis_index("block")
    side = lax.rem(chain, 2)
    sib = chain + 1 - 2 * side
    first = block * own.shape[1] + side * 2
    has_prev = block > 0
    has_next = block < blocks - 1
    even = side == 0
    odd = side == 1
    barrier = pltpu.get_barrier_semaphore()
    signal_to(barrier, sib, block)
    pl.when(has_next)(lambda: signal_to(barrier, chain, block + 1))
    pl.when(has_prev)(lambda: signal_to(barrier, chain, block - 1))
    pl.when(even & has_prev)(lambda: signal_to(barrier, sib, block - 1))
    pl.when(odd & has_next)(lambda: signal_to(barrier, sib, block + 1))
    prev_count = has_prev.astype(jnp.int32)
    next_count = has_next.astype(jnp.int32)
    pl.semaphore_wait(barrier, 1 + (2 - side) * prev_count + (1 + side) * next_count)

    def remote(src, dst, k, to_chain, to_block):
        return pltpu.make_async_remote_copy(
            src_ref=src,
            dst_ref=dst,
            send_sem=send_sems.at[k],
            recv_sem=recv_sems.at[k],
            device_id={"chain": to_chain, "block": to_block},
            device_id_type=MESH,
        )

    edge_next = remote(own.at[0, 3], outer, 0, chain, block + 1)
    edge_prev = remote(own.at[0, 0, 0], outer.at[0], 1, chain, block - 1)
    edge_low = remote(own.at[0, 3, 1], lower, 2, sib, block + 1)
    to_odd = remote(own.at[0, pl.ds(1, 3)], other, 3, sib, block)
    to_even = remote(own.at[0, pl.ds(0, 3)], other, 3, sib, block)
    rows = [
        remote(sizes, sib_sizes, 4, sib, block),
        remote(counts, sib_counts, 5, sib, block),
        remote(terms, sib_terms, 6, sib, block),
    ]
    pl.when(even & has_next)(edge_next.start)
    pl.when(odd & has_next)(edge_low.start)
    pl.when(odd & has_prev)(edge_prev.start)
    for copy in rows:
        copy.start()
    pl.when(even)(to_odd.start)
    pl.when(odd)(to_even.start)

    @pl.when((even & (block == 0)) | (odd & (block == blocks - 1)))
    def _():
        outer[...] = jnp.zeros_like(outer)

    @pl.when(even & (block == 0))
    def _():
        lower[...] = jnp.zeros_like(lower)

    sketch_t[...] = sketch[...].astype(jnp.float32).T.astype(jnp.bfloat16)
    for copy in rows:
        copy.wait()

    def entry(row, index):
        lane = lax.broadcasted_iota(jnp.int32, row.shape, 1)
        return jnp.sum(jnp.where(lane == index, row.astype(jnp.float32), 0.0), axis=1, keepdims=True)

    def write_row(ref, count_row, term_row):
        hopping, ising, field = (term_row[:, i : i + 1] for i in range(3))
        rotation = 0.5 * tau_step * hopping
        middle = jnp.exp(0.25 * tau_step * ising)
        grow, shrink = jnp.exp(rotation), jnp.exp(-rotation)
        values = [
            entry(count_row, first),
            entry(count_row, first + 1),
            jnp.exp(-tau_step * (0.25 * ising - 0.5 * field)),
            middle * (0.5 * (grow + shrink)),
            -middle * (0.5 * (grow - shrink)),
            jnp.exp(-tau_step * (0.25 * ising + 0.5 * field)),
        ]
        lane = lax.broadcasted_iota(jnp.int32, ref.shape, 1)
        result = jnp.zeros(ref.shape, jnp.float32)
        for i, value in enumerate(values):
            result = jnp.where(lane == i, jnp.broadcast_to(value, ref.shape), result)
        ref[...] = result

    def pick(take, first_row, second_row):
        return jnp.where(take, first_row.astype(jnp.float32), second_row.astype(jnp.float32))

    write_row(
        even_row,
        pick(even, counts[0, 1:2, :], counts[0, 0:1, :]),
        pick(even, terms[0, 1:2, :], terms[0, 0:1, :]),
    )
    write_row(
        odd_row,
        pick(odd, counts[0, 1:2, :], sib_counts[0, 1:2, :]),
        pick(odd, terms[0, 1:2, :], sib_terms[0, 1:2, :]),
    )
    lefts = [pick(even, sizes[0, i : i + 1, :], sib_sizes[0, i : i + 1, :]) for i in range(2)]
    rights = [pick(odd, sizes[0, i : i + 1, :], sib_sizes[0, i : i + 1, :]) for i in range(2)]
    row = lax.broadcasted_iota(jnp.int32, (size, size), 0).astype(jnp.float32)
    column = lax.broadcasted_iota(jnp.int32, (size, size), 1).astype(jnp.float32)

    def cut(value, bond, sector, shift):
        keep = (row < entry(bond[0], sector)) & (column < entry(bond[1], sector + shift))
        return jnp.where(keep, value.astype(jnp.float32), 0.0).astype(jnp.bfloat16)

    def put_left(k, value):
        for s in range(2):
            left[k, s] = cut(value(s), lefts, first - 1 + k, s)

    def put_top(k, value):
        top[k] = cut(value, rights, first + k, 0)

    def put_low(k, value):
        low[k] = cut(value, rights, first - 1 + k, 1)

    @pl.when(even)
    def _():
        put_left(1, lambda s: own[0, 0, s])
        put_left(2, lambda s: own[0, 1, s])
        to_odd.wait()
        for i in range(3):
            put_top(i, other[i, 0])
        for i in range(2):
            put_low(i + 1, other[i, 1])
        pl.when(has_prev)(edge_next.wait_recv)
        pl.when(has_prev)(edge_low.wait_recv)
        put_left(0, lambda s: outer[s])
        put_low(0, lower[...])
        pl.when(has_next)(edge_next.wait_send)

    @pl.when(odd)
    def _():
        for i in range(3):
            put_low(i, own[0, i + 1, 1])
        for i in range(2):
            put_top(i, own[0, i + 2, 0])
        to_even.wait()
        for i in range(3):
            put_left(i, lambda s: other[i, s])
        pl.when(has_next)(edge_prev.wait_recv)
        put_top(2, outer[0])
        pl.when(has_prev)(edge_prev.wait_send)
        pl.when(has_next)(edge_low.wait_send)


def step_kernel(chips, blocks, target, left_ref, top_ref, low_ref, sketch_t, even_row, odd_row, out, *refs):
    (two_ref, sample_ref, tri_a, tri_b, basis_ref, coef_ref, far_ref, edge_ref) = refs[:8]
    (sib_ref, bot_ref, part_ref, norm_ref, sum_ref, scale_ref, send_sems, recv_sems, nsend, nrecv, turn) = refs[8:]
    size = bot_ref.shape[0]
    chain = lax.axis_index("chain")
    block = lax.axis_index("block")
    side = lax.rem(chain, 2)
    sib = chain + 1 - 2 * side
    sites = 2 * chips
    has_prev = block > 0
    has_next = block < blocks - 1
    even = side == 0
    odd = side == 1
    back = lax.rem(chain + sites - 2, sites)
    ahead = lax.rem(chain + 2, sites)
    ahead_even = lax.rem(chain + 2 - side, sites)
    back_odd = lax.rem(chain + sites - 1, sites)
    group = 2 * blocks
    me = side * blocks + block
    barrier = pltpu.get_barrier_semaphore()

    def peer(step):
        index = lax.rem(me + step, group)
        return index, chain - side + index // blocks, lax.rem(index, blocks)

    for step in range(1, group):
        _, to_chain, to_block = peer(step)
        signal_to(barrier, to_chain, to_block)
    signal_to(barrier, back, block)

    @pl.when(even)
    def _():
        signal_to(barrier, back_odd, block)
        signal_to(barrier, ahead, block)

    @pl.when(odd)
    def _():
        signal_to(barrier, ahead, block)
        signal_to(barrier, ahead_even, block)

    def remote(src, dst, k, to_chain, to_block):
        return pltpu.make_async_remote_copy(
            src_ref=src,
            dst_ref=dst,
            send_sem=send_sems.at[k],
            recv_sem=recv_sems.at[k],
            device_id={"chain": to_chain, "block": to_block},
            device_id_type=MESH,
        )

    def norm_copy(layer, step):
        index, to_chain, to_block = peer(step)
        return pltpu.make_async_remote_copy(
            src_ref=norm_ref.at[layer, me],
            dst_ref=norm_ref.at[layer, me],
            send_sem=nsend.at[layer, step],
            recv_sem=nrecv.at[layer, me],
            device_id={"chain": to_chain, "block": to_block},
            device_id_type=MESH,
        )

    def norm_arrival(layer, step):
        index, to_chain, to_block = peer(step)
        return pltpu.make_async_remote_copy(
            src_ref=norm_ref.at[layer, index],
            dst_ref=norm_ref.at[layer, index],
            send_sem=nsend.at[layer, step],
            recv_sem=nrecv.at[layer, index],
            device_id={"chain": to_chain, "block": to_block},
            device_id_type=MESH,
        )

    def share_norm(layer):
        norm_ref[layer, me] = part_ref[...]
        for step in range(1, group):
            norm_copy(layer, step).start()

    def norm_scale(layer):
        for step in range(1, group):
            norm_arrival(layer, step).wait_recv()
        total = norm_ref[layer, 0]
        for i in range(1, group):
            total = total + norm_ref[layer, i]
        return jnp.sqrt(target / total)

    @pl.when(even & (block == 0))
    def _():
        edge_ref[...] = jnp.zeros_like(edge_ref)

    @pl.when(odd & (block == blocks - 1))
    def _():
        far_ref[2] = jnp.zeros_like(far_ref[2])

    @pl.when(odd & (block == blocks - 1))
    def _():
        bot_ref[...] = jnp.zeros_like(bot_ref)

    def row_terms(ref):
        terms = [ref[0:1, i : i + 1] for i in range(6)]
        return terms[:2], terms[2:]

    far = [remote(basis_ref.at[0, i], far_ref.at[i], i, back, block) for i in range(2)]
    edge_even = remote(coef_ref.at[0, 1], edge_ref, 2, sib, block)
    edge_odd = remote(coef_ref.at[0, 1], edge_ref, 2, sib, block + 1)
    pass_even = remote(far_ref.at[0], far_ref.at[2], 3, sib, block - 1)
    pass_odd = remote(far_ref.at[0], far_ref.at[2], 3, sib, block)

    first_turn = even

    def before_even(i):
        pass

    def sent_even(i):
        if i == 0:
            pl.semaphore_wait(barrier, group + 2)
        if i == 0:
            far[i].start()
        else:
            pl.when(first_turn)(far[i].start)
        if i == 1:
            pl.when(even)(edge_even.start)
            pl.when(odd & has_next)(edge_odd.start)

    scratch = (two_ref, sample_ref, (tri_a, tri_b))
    ranks, weights = row_terms(even_row)
    update_sectors(
        lambda k, s: left_ref[k, s],
        lambda k: top_ref[k],
        lambda k: low_ref[k],
        NN,
        sketch_t,
        ranks,
        weights,
        basis_ref.at[0],
        coef_ref.at[0],
        part_ref,
        scratch,
        before_even,
        sent_even,
    )
    share_norm(0)
    far[0].wait_recv()
    pl.when(even & has_prev)(pass_even.start)
    pl.when(odd)(pass_odd.start)

    @pl.when(even)
    def _():
        far[0].wait_send()
        far[1].wait_send()
        signal_to(turn, sib, block)

    @pl.when(odd)
    def _():
        pl.semaphore_wait(turn, 1)
        far[1].start()

    scale = norm_scale(0)[0:1, 0:1]
    pl.when(odd | has_prev)(edge_even.wait_recv)

    def before_odd(i):
        if i == 0:
            far[1].wait_recv()
        else:
            pl.when(even | has_next)(pass_even.wait_recv)

    lefts = (edge_ref, coef_ref.at[0, 0], coef_ref.at[0, 1])
    ranks, weights = row_terms(odd_row)
    new_even, new_odd = [], []
    for i in range(2):
        for half in range(2):
            piece = coef_ref.at[1, i, :, pl.ds(half * size, size)]
            k = 2 * i + half
            new_even.append(remote(piece, out.at[0, i, half], 4 + k, ahead, block))
            new_odd.append(remote(piece, out.at[0, 2 + i, half], 8 + k, ahead_even, block))
    sibs = [remote(basis_ref.at[1, i], sib_ref.at[i], 12 + i, sib, block) for i in range(2)]
    bot = remote(basis_ref.at[1, 0, :, pl.ds(size, size)], bot_ref, 14, sib, block - 1)

    def sent_odd(i):
        for k in (2 * i, 2 * i + 1):
            pl.when(even)(new_even[k].start)
            pl.when(odd)(new_odd[k].start)
        pl.when(even)(sibs[i].start)
        if i == 1:
            pl.when(even & has_prev)(bot.start)

    update_sectors(
        lambda k, s: lefts[k][:, s * size : (s + 1) * size],
        lambda k: far_ref[k, :, :size],
        lambda k: far_ref[k, :, size:],
        NT,
        sketch_t,
        ranks,
        [w * scale for w in weights],
        basis_ref.at[1],
        coef_ref.at[1],
        part_ref,
        scratch,
        before_odd,
        sent_odd,
    )
    share_norm(1)
    sum_ref[...] = norm_scale(1)
    scale_copy = remote(sum_ref, scale_ref, 15, ahead, block)
    pl.when(even)(scale_copy.start)

    @pl.when(even)
    def _():
        for k in range(4):
            new_even[k].wait_recv()
            new_odd[k].wait_recv()
        scale_copy.wait_recv()
        scale = scale_ref[0:1, 0:1]
        for i in range(4):
            for half in range(2):
                out[0, i, half] = (out[0, i, half].astype(jnp.float32) * scale).astype(jnp.bfloat16)

    @pl.when(odd)
    def _():
        def flip(blocked):
            return blocked.astype(jnp.float32).T.astype(jnp.bfloat16)

        for i in range(2):
            sibs[i].wait_recv()
        pl.when(has_next)(bot.wait_recv)
        for i in range(4):
            basis = sib_ref[i] if i < 2 else basis_ref[1, i - 2]
            out[0, i, 0] = flip(basis[:, :size])
            if i > 0:
                out[0, i - 1, 1] = flip(basis[:, size:])
        out[0, 3, 1] = flip(bot_ref[...])

    pl.when(odd)(far[0].wait_send)
    pl.when(odd)(far[1].wait_send)
    for k in range(4):
        pl.when(even)(new_even[k].wait_send)
        pl.when(odd)(new_odd[k].wait_send)
    for i in range(2):
        pl.when(even)(sibs[i].wait_send)
    pl.when(even | has_next)(edge_even.wait_send)
    pl.when(odd | has_prev)(pass_even.wait_send)
    pl.when(even & has_prev)(bot.wait_send)
    pl.when(even)(scale_copy.wait_send)
    for layer in range(2):
        for step in range(1, group):
            norm_copy(layer, step).wait_send()


def body(sites, blocks, site_tensors, sketch, bond_sizes, kept_ranks, couplings):
    sector_count = site_tensors.shape[1]
    size = site_tensors.shape[-1]
    bf16 = jnp.bfloat16
    f32 = jnp.float32
    row = jax.ShapeDtypeStruct((8, 128), f32)
    terms = pl.pallas_call(
        functools.partial(entry_kernel, blocks),
        out_shape=[
            jax.ShapeDtypeStruct((3, 2, size, size), bf16),
            jax.ShapeDtypeStruct((3, size, size), bf16),
            jax.ShapeDtypeStruct((3, size, size), bf16),
            jax.ShapeDtypeStruct((size, 2 * size), bf16),
            row,
            row,
        ],
        in_specs=[VMEM] * 5,
        out_specs=[VMEM] * 6,
        scratch_shapes=[
            pltpu.VMEM((3, 2, size, size), bf16),
            pltpu.VMEM((2, size, size), bf16),
            pltpu.VMEM((size, size), bf16),
            pltpu.VMEM(bond_sizes.shape, jnp.int32),
            pltpu.VMEM(kept_ranks.shape, jnp.int32),
            pltpu.VMEM(couplings.shape, f32),
            pltpu.SemaphoreType.DMA((7,)),
            pltpu.SemaphoreType.DMA((7,)),
        ],
        compiler_params=pltpu.CompilerParams(collective_id=0, has_side_effects=True),
        name="entry",
    )(site_tensors, sketch, bond_sizes, kept_ranks, couplings)
    target = float(sector_count * blocks * size * size)
    group = 2 * blocks
    return pl.pallas_call(
        functools.partial(step_kernel, sites // 2, blocks, target),
        out_shape=jax.ShapeDtypeStruct(site_tensors.shape, bf16),
        in_specs=[VMEM] * 6,
        out_specs=VMEM,
        scratch_shapes=[
            pltpu.VMEM((2, 2 * size, 2 * size), bf16),
            pltpu.VMEM((2, size, 2 * size), f32),
            pltpu.VMEM((size, size), f32),
            pltpu.VMEM((size, size), f32),
            pltpu.VMEM((2, 2, size, 2 * size), bf16),
            pltpu.VMEM((2, 2, size, 2 * size), bf16),
            pltpu.VMEM((3, size, 2 * size), bf16),
            pltpu.VMEM((size, 2 * size), bf16),
            pltpu.VMEM((2, size, 2 * size), bf16),
            pltpu.VMEM((size, size), bf16),
            pltpu.VMEM((8, 128), f32),
            pltpu.VMEM((2, group, 8, 128), f32),
            pltpu.VMEM((8, 128), f32),
            pltpu.VMEM((8, 128), f32),
            pltpu.SemaphoreType.DMA((16,)),
            pltpu.SemaphoreType.DMA((16,)),
            pltpu.SemaphoreType.DMA((2, group)),
            pltpu.SemaphoreType.DMA((2, group)),
            pltpu.SemaphoreType.REGULAR,
        ],
        compiler_params=pltpu.CompilerParams(collective_id=1, has_side_effects=True),
        name="step",
    )(*terms)


def solution(mesh):
    placed = (
        P("chain", "block", None, None, None),
        P(),
        P("chain", None, None),
        P("chain", None, None),
        P("chain", None, None),
    )
    return jax.shard_map(
        functools.partial(body, mesh.shape["chain"], mesh.shape["block"]),
        mesh=mesh,
        in_specs=placed,
        out_specs=P("chain", "block", None, None, None),
        check_vma=False,
    )
```
